128 devices in a mesh: gx: 16 (over z, y), yz: 8 (over x, core).
Axes of the slice: x: 4, y: 4, z: 4, core: 2. Of those that a mesh axis runs over, the one named last changes fastest.
Arguments:
- cell_matrix: bfloat16 [32, 256, 256, 256], P('gx', 'yz'), as said below
- x_coupling: bfloat16 [32, 256, 128], P('gx', 'yz'), may hold values from 0.5 to 2
- y_coupling: bfloat16 [32, 256, 128], P('gx', 'yz'), may hold values from 0.5 to 2
- cell_interp: bfloat16 [32, 256, 256, 128], P('gx', 'yz'), may hold values from -0.375 to 0.375
- cell_skel: int32 [32, 256, 128], P('gx', 'yz'), may hold values from 0 to 255, as said below
- cell_rank: int32 [32, 256], P('gx', 'yz'), may hold values from 64 to 128, as said below
- x_face_interp: bfloat16 [32, 256, 256, 128], P('gx', 'yz'), may hold values from -0.375 to 0.375
- x_face_skel: int32 [32, 256, 128], P('gx', 'yz'), may hold values from 0 to 255, as said below
- x_face_rank: int32 [32, 256], P('gx', 'yz'), may hold values from 64 to 128, as said below
- y_face_interp: bfloat16 [32, 256, 256, 128], P('gx', 'yz'), may hold values from -0.375 to 0.375
- y_face_skel: int32 [32, 256, 128], P('gx', 'yz'), may hold values from 0 to 255, as said below
- y_face_rank: int32 [32, 256], P('gx', 'yz'), may hold values from 64 to 128, as said below
Outputs:
- x_face_block: bfloat16 [32, 256, 128, 128], P('gx', 'yz')
- y_face_block: bfloat16 [32, 256, 128, 128], P('gx', 'yz')
The draws below stay inside these ranges and needn't reach their ends.
Inputs may be any that keep to these rules, and one draw needn't show every extreme that they name: `cell_skel`: each row names 128 distinct unknowns of a cell block. `cell_rank`: the slots of cell_skel below a cell's rank are its live skeleton. `x_face_skel`: each row names 128 distinct unknowns of the face's two cells. `x_face_rank`: the slots of x_face_skel below a face's rank are its live skeleton. `y_face_skel`: each row names 128 distinct unknowns of the face's two cells. `y_face_rank`: the slots of y_face_skel below a face's rank are its live skeleton. `cell_matrix`: symmetric.
All inputs are finite; a program needn't handle non-finite values.
Results may differ from the reference program's by a relative error of at most 0.0053.
Values may be sent and summed in bfloat16 or wider, within the bound.
A program may use at most 128 MiB of HBM per device.

```python
import math
import jax
import jax.numpy as jnp
from jax import lax

B = 256
K = 128
KF = 128
NXC = 32
NYZ = 256


def draw_cell_matrix(key, part):
    first_key, second_key = jax.random.split(jax.random.fold_in(key, 7))
    noise = jax.random.normal(first_key, (NXC, NYZ, B, B), jnp.float32)
    diagonal = jax.random.uniform(second_key, (NXC, NYZ, B), jnp.float32, 1.0, 2.0)
    symmetric = (noise + jnp.swapaxes(noise, -1, -2)) * (0.35 / math.sqrt(B))
    return (symmetric + diagonal[..., None] * jnp.eye(B, dtype=jnp.float32)).astype(jnp.bfloat16)


def skeleton_lists(key, slot_total, pool_size):
    keys = jax.random.split(key, NXC * NYZ)

    def choose_slots(single_key):
        return jax.random.permutation(single_key, pool_size)[:slot_total]
    chosen = jax.vmap(choose_slots)(keys)
    return chosen.reshape(NXC, NYZ, slot_total).astype(jnp.int32)


def rank_values(key, slot_total):
    ranks = jax.random.randint(key, (NXC, NYZ), slot_total // 2, slot_total + 1, dtype=jnp.int32)
    return ranks.at[0, 0].set(slot_total).at[NXC - 1, NYZ - 1].set(slot_total // 2)


def draw_cell_skel(key, part):
    return skeleton_lists(jax.random.fold_in(key, 11), K, B)


def draw_cell_rank(key, part):
    return rank_values(jax.random.fold_in(key, 13), K)


def draw_x_face_skel(key, part):
    return skeleton_lists(jax.random.fold_in(key, 17), KF, 2 * K)


def draw_x_face_rank(key, part):
    return rank_values(jax.random.fold_in(key, 19), KF)


def draw_y_face_skel(key, part):
    return skeleton_lists(jax.random.fold_in(key, 23), KF, 2 * K)


def draw_y_face_rank(key, part):
    return rank_values(jax.random.fold_in(key, 29), KF)


def level_of(stream_key, shape, pieces, smallest, high):
    loudness, own = 1.0, jax.random.fold_in(stream_key, 6)
    for position, parts in pieces:
        heights = jnp.exp(jax.random.uniform(jax.random.fold_in(own, position), (parts,), jnp.float32, smallest / len(pieces), high / len(pieces)))
        loudness = loudness * jnp.repeat(heights, shape[position] // parts).reshape([-1 if axis == position else 1 for axis in range(len(shape))])
    return loudness


def normal_values(key, shape, deviation, most, shards=(), kind=jnp.bfloat16):
    factor_of = level_of(key, shape, shards, -0.22, 0.18) if shards else 1.0
    array = jax.random.normal(key, shape, jnp.float32) * deviation * factor_of
    return jnp.minimum(jnp.maximum(array, -most), most).astype(kind)


def setup_inputs(seed: int = 0) -> dict:
    splits = jax.random.split(jax.random.key(seed), 13)
    cell_matrix = draw_cell_matrix(jax.random.fold_in(splits[12], 71), 0)
    x_coupling = jnp.clip(jnp.exp(math.log(2.0) - 1.3862944 * jax.random.uniform(splits[1], (NXC, NYZ, B // 2), jnp.float32) ** level_of(splits[1], (NXC, NYZ, B // 2), ((0, 16), (1, 8)), -0.2, 0.2)), 0.5, 2.0).astype(jnp.bfloat16)
    y_coupling = jnp.clip(jnp.exp(math.log(2.0) - 1.3862944 * jax.random.uniform(splits[2], (NXC, NYZ, B // 2), jnp.float32) ** level_of(splits[2], (NXC, NYZ, B // 2), ((0, 16), (1, 8)), -0.2, 0.2)), 0.5, 2.0).astype(jnp.bfloat16)
    cell_interp = normal_values(splits[3], (NXC, NYZ, B, K), B ** -0.5, 0.375, ((0, 16), (1, 8)))
    cell_skel = draw_cell_skel(jax.random.fold_in(splits[12], 71), 0)
    cell_rank = draw_cell_rank(jax.random.fold_in(splits[12], 71), 0)
    x_face_interp = normal_values(splits[6], (NXC, NYZ, 2 * K, KF), (2 * K) ** -0.5, 0.375, ((0, 16), (1, 8)))
    x_face_skel = draw_x_face_skel(jax.random.fold_in(splits[12], 71), 0)
    x_face_rank = draw_x_face_rank(jax.random.fold_in(splits[12], 71), 0)
    y_face_interp = normal_values(splits[9], (NXC, NYZ, 2 * K, KF), (2 * K) ** -0.5, 0.375, ((0, 16), (1, 8)))
    y_face_skel = draw_y_face_skel(jax.random.fold_in(splits[12], 71), 0)
    y_face_rank = draw_y_face_rank(jax.random.fold_in(splits[12], 71), 0)
    return dict(cell_matrix=cell_matrix, x_coupling=x_coupling, y_coupling=y_coupling, cell_interp=cell_interp, cell_skel=cell_skel, cell_rank=cell_rank, x_face_interp=x_face_interp, x_face_skel=x_face_skel, x_face_rank=x_face_rank, y_face_interp=y_face_interp, y_face_skel=y_face_skel, y_face_rank=y_face_rank)


def make_basis(skel_list, rank_list, interp):
    row_count = interp.shape[-2]
    slot_count = skel_list.shape[-1]
    slot_index = lax.broadcasted_iota(jnp.int32, skel_list.shape, skel_list.ndim - 1)
    live_slots = slot_index < rank_list[..., None]
    row_index = lax.broadcasted_iota(jnp.int32, skel_list.shape[:-1] + (row_count, slot_count), skel_list.ndim - 1)
    picked_rows = (row_index == skel_list[..., None, :]) & live_slots[..., None, :]
    kept_rows = jnp.any(picked_rows, axis=-1, keepdims=True)
    interp_part = jnp.where(live_slots[..., None, :], interp.astype(jnp.float32), jnp.float32(0.0))
    return jnp.where(picked_rows, jnp.float32(1.0), jnp.where(kept_rows, jnp.float32(0.0), interp_part)).astype(jnp.bfloat16)


def project(matrix, left_basis, right_basis):
    inner_prod = jnp.einsum('...ij,...jk->...ik', matrix.astype(jnp.float32), right_basis.astype(jnp.float32)).astype(jnp.bfloat16)
    inner_prod = lax.optimization_barrier(inner_prod)
    return jnp.einsum('...ji,...jk->...ik', left_basis.astype(jnp.float32), inner_prod.astype(jnp.float32))


def coupling_link(conduct, own_basis, right_basis):
    half_rows = own_basis.shape[-2] // 2
    scaled = (-conduct.astype(jnp.float32)[..., None] * right_basis[..., :half_rows, :].astype(jnp.float32)).astype(jnp.bfloat16)
    scaled = lax.optimization_barrier(scaled)
    return jnp.einsum('...ji,...jk->...ik', own_basis[..., half_rows:, :].astype(jnp.float32), scaled.astype(jnp.float32))


def face_matrix(left_block, link_block, right_block):
    upper_half = jnp.concatenate([left_block, link_block], axis=-1)
    lower_half = jnp.concatenate([jnp.swapaxes(link_block, -1, -2), right_block], axis=-1)
    return jnp.concatenate([upper_half, lower_half], axis=-2)


def cell_row(packed):
    matrix, x_edge, y_edge, own_basis, right_x, right_y = packed
    schur_block = project(matrix, own_basis, own_basis).astype(jnp.bfloat16)
    x_link = coupling_link(x_edge, own_basis, right_x).astype(jnp.bfloat16)
    y_link = coupling_link(y_edge, own_basis, right_y).astype(jnp.bfloat16)
    return schur_block, x_link, y_link


def face_row(packed):
    left_block, link_block, right_block, face_basis = packed
    return project(face_matrix(left_block, link_block, right_block), face_basis, face_basis).astype(jnp.bfloat16)


def reference(cell_matrix, x_coupling, y_coupling, cell_interp, cell_skel, cell_rank, x_face_interp, x_face_skel, x_face_rank, y_face_interp, y_face_skel, y_face_rank):
    cell_basis = make_basis(cell_skel, cell_rank, cell_interp)
    next_x = jnp.concatenate([cell_basis[1:], jnp.zeros_like(cell_basis[:1])], axis=0)
    next_y = jnp.concatenate([cell_basis[:, 1:], jnp.zeros_like(cell_basis[:, :1])], axis=1)
    schur_block, x_link, y_link = lax.map(cell_row, (cell_matrix, x_coupling, y_coupling, cell_basis, next_x, next_y))
    schur_x = jnp.concatenate([schur_block[1:], jnp.zeros_like(schur_block[:1])], axis=0)
    schur_y = jnp.concatenate([schur_block[:, 1:], jnp.zeros_like(schur_block[:, :1])], axis=1)
    x_basis = make_basis(x_face_skel, x_face_rank, x_face_interp)
    y_basis = make_basis(y_face_skel, y_face_rank, y_face_interp)
    x_face_block = lax.map(face_row, (schur_block, x_link, schur_x, x_basis))
    y_face_block = lax.map(face_row, (schur_block, y_link, schur_y, y_basis))
    return x_face_block, y_face_block
```

```python
import functools

import jax
import jax.numpy as jnp
from jax import lax
from jax.experimental import pallas as pl
from jax.experimental.pallas import tpu as pltpu
from jax.sharding import PartitionSpec as P

F32, BF16 = jnp.float32, jnp.bfloat16
ROWS = (((1,), (1,)), ((), ()))
CB = 8
CM = 4


def passed_along(x, axis, by):
    devices = lax.axis_size(axis)
    pairs = [(i, i + by) for i in range(devices) if 0 <= i + by < devices]
    return lax.ppermute(x, axis, pairs)


def dot(a, b):
    return jnp.dot(a, b, preferred_element_type=F32)


def dot_t(a, b):
    return lax.dot_general(a, b, ROWS, preferred_element_type=F32)


def basis_t(column, interp):
    across = interp.T.astype(F32)
    lanes = lax.broadcasted_iota(jnp.int32, across.shape, 1).astype(F32)
    picked = lanes == column
    kept = jnp.max(jnp.where(picked, 1.0, 0.0), axis=0, keepdims=True)
    rest = jnp.where((kept > 0.0) | (column < 0.0), 0.0, across)
    return jnp.where(picked, 1.0, rest).astype(BF16)


def schur_t(basis, matrix):
    inner = dot(basis, matrix).astype(BF16)
    return dot_t(inner, basis).astype(BF16)


def link_of(own_bottom, conduct, right_top):
    scaled = (right_top.astype(F32) * -conduct).astype(BF16)
    return dot_t(own_bottom, scaled).astype(BF16)


def face_of(basis, left_t, link, right_t):
    upper = jnp.concatenate([left_t, link], axis=1)
    lower = jnp.concatenate([link.T, right_t], axis=1)
    inner = dot(basis, jnp.concatenate([upper, lower], axis=0)).astype(BF16)
    return dot_t(basis, inner).astype(BF16)


def columns_of(lists):
    return lists.T


def row_basis_kernel(list_ref, interp_ref, basis_ref, top_ref):
    columns = columns_of(list_ref[...])
    for c in range(CB):
        basis = basis_t(columns[:, c : c + 1], interp_ref[c])
        basis_ref[c] = basis
        top_ref[c] = basis[:, :128]


def packed_into(out_ref, at, first, second):
    down = lax.broadcasted_iota(jnp.int32, (128, 128), 0)
    across = lax.broadcasted_iota(jnp.int32, (128, 128), 1)
    out_ref[at * 128 : at * 128 + 128] = jnp.where(down <= across, first, second)
    diagonal = jnp.where(down == across, second.astype(F32), 0.0)
    return jnp.sum(diagonal, axis=0, keepdims=True)


def row_schur_kernel(
    basis_ref, matrix_ref, list_ref, interp_ref, corner_ref, schur_ref, early_ref, late_ref, edge_ref
):
    step = pl.program_id(0)
    blocks = [schur_t(basis_ref[c], matrix_ref[c]) for c in range(CB)]
    for c in range(CB):
        schur_ref[c] = blocks[c]

    def pack(out_ref):
        rows = [packed_into(out_ref, at, blocks[2 * at], blocks[2 * at + 1]) for at in range(CB // 2)]
        rows.append(jnp.zeros((16 - CB // 2, 128), F32))
        out_ref[CB // 2 * 128 :] = jnp.concatenate(rows, axis=0).astype(BF16)

    @pl.when(step < 3)
    def _():
        pack(early_ref)

    @pl.when(step == 3)
    def _():
        pack(late_ref)

    @pl.when(step == 0)
    def _():
        edge_ref[0, :128] = basis_ref[0, :, :128]
        edge_ref[0, 128:] = blocks[0]
        basis = basis_t(columns_of(list_ref[...])[:, :1], interp_ref[...])
        edge_ref[1, :128] = basis[:, :128]
        edge_ref[1, 128:] = schur_t(basis, corner_ref[...])


def main_kernel(
    list_ref,
    basis0_ref,
    schur0_ref,
    matrix_ref,
    interp_ref,
    x_interp_ref,
    y_interp_ref,
    x_conduct_ref,
    y_conduct_ref,
    x_face_ref,
    y_face_ref,
    bottom1_ref,
    schur1_ref,
    x_basis1_ref,
    next_top,
    next_schur,
):
    lists = columns_of(list_ref[...])

    def column(kind, row, c):
        at = (kind * 2 + row) * CM + c
        return lists[:, at : at + 1]

    tops = [[None] * CM, [None] * CM]
    bottoms = [[None] * CM, [None] * CM]
    schurs = [[None] * CM, [None] * CM]
    for c in range(CM):
        basis = basis_t(column(0, 1, c), interp_ref[c])
        block = schur_t(basis, matrix_ref[c])
        tops[1][c], bottoms[1][c], schurs[1][c] = basis[:, :128], basis[:, 128:], block
        bottom1_ref[c] = basis[:, 128:]
        schur1_ref[c] = block
        tops[0][c], bottoms[0][c] = basis0_ref[c, :, :128], basis0_ref[c, :, 128:]
        schurs[0][c] = schur0_ref[c]
        x_basis1_ref[c] = basis_t(column(1, 1, c), x_interp_ref[1, c])
    for c in range(CM):
        link = link_of(bottoms[0][c], x_conduct_ref[c : c + 1], tops[1][c])
        x_basis = basis_t(column(1, 0, c), x_interp_ref[0, c])
        x_face_ref[c] = face_of(x_basis, schurs[0][c], link, schurs[1][c])
        for row in range(2):
            last = c == CM - 1
            right_top = next_top[row] if last else tops[row][c + 1]
            right_schur = next_schur[row] if last else schurs[row][c + 1]
            at = row * CM + c
            link = link_of(bottoms[row][c], y_conduct_ref[at : at + 1], right_top)
            y_basis = basis_t(column(2, row, c), y_interp_ref[row, c])
            y_face_ref[row, c] = face_of(y_basis, schurs[row][c], link, right_schur)
    for row in range(2):
        next_top[row] = tops[row][0]
        next_schur[row] = schurs[row][0]


def edge_kernel(
    list_ref, bottom0_ref, bottom1_ref, schur0_ref, schur1_ref, edge_ref, interp_ref, conduct_ref, face_in, face_ref
):
    del face_in
    lists = columns_of(list_ref[...])
    for row, (bottom_ref, schur_ref) in enumerate(((bottom0_ref, schur0_ref), (bottom1_ref, schur1_ref))):
        link = link_of(bottom_ref[...], conduct_ref[row : row + 1], edge_ref[row, :128])
        basis = basis_t(lists[:, row : row + 1], interp_ref[row])
        face_ref[row] = face_of(basis, schur_ref[...], link, edge_ref[row, 128:])


def last_kernel(bottom_ref, schur_ref, basis_ref, conduct_ref, top_ref, packed_ref, face_in, face_ref):
    del face_in
    down = lax.broadcasted_iota(jnp.int32, (128, 128), 0)
    across = lax.broadcasted_iota(jnp.int32, (128, 128), 1)
    for at in range(CB // 2):
        packed = packed_ref[at * 128 : at * 128 + 128]
        turned = packed.T
        diagonal = packed_ref[CB // 2 * 128 : CB // 2 * 128 + 16][at : at + 1]
        first = jnp.where(down <= across, packed, turned)
        second = jnp.where(down > across, packed, turned)
        second = jnp.where(down == across, jnp.broadcast_to(diagonal, (128, 128)), second)
        for c, right in ((2 * at, first), (2 * at + 1, second)):
            link = link_of(bottom_ref[c], conduct_ref[c : c + 1], top_ref[c])
            face_ref[c] = face_of(basis_ref[c], schur_ref[c], link, right)


PARAMS = pltpu.CompilerParams(vmem_limit_bytes=48 << 20)


def cost(flops, size):
    return pl.CostEstimate(flops=flops, bytes_accessed=size, transcendentals=0)


def spec(*args):
    return pl.BlockSpec(*args)


def shape(*sizes):
    return jax.ShapeDtypeStruct(sizes, BF16)


def body(
    cell_matrix,
    x_coupling,
    y_coupling,
    cell_interp,
    cell_skel,
    cell_rank,
    x_face_interp,
    x_face_skel,
    x_face_rank,
    y_face_interp,
    y_face_skel,
    y_face_rank,
):
    def marked(skel, rank):
        slots = lax.broadcasted_iota(jnp.int32, skel.shape, 2)
        return jnp.where(slots < rank[..., None], skel, -1).astype(F32)

    NJ = cell_skel.shape[1]
    cell_list = marked(cell_skel, cell_rank)
    x_list = marked(x_face_skel, x_face_rank)
    y_list = marked(y_face_skel, y_face_rank)

    basis0, top0 = pl.pallas_call(
        row_basis_kernel,
        grid=(NJ // CB,),
        in_specs=[
            spec((None, CB, 128), lambda j: (0, j, 0)),
            spec((None, CB, 256, 128), lambda j: (0, j, 0, 0)),
        ],
        out_specs=[spec((CB, 128, 256), lambda j: (j, 0, 0)), spec((CB, 128, 128), lambda j: (j, 0, 0))],
        out_shape=[shape(NJ, 128, 256), shape(NJ, 128, 128)],
        compiler_params=PARAMS,
        cost_estimate=cost(1 << 24, 5 << 20),
        name="row_basis",
    )(cell_list, cell_interp)
    top_in = passed_along(top0, "gx", -1)

    packed = (CB // 2) * 128 + 16
    schur0, early, late, edge = pl.pallas_call(
        row_schur_kernel,
        grid=(NJ // CB,),
        in_specs=[
            spec((CB, 128, 256), lambda j: (j, 0, 0)),
            spec((None, CB, 256, 256), lambda j: (0, j, 0, 0)),
            spec((None, 8, 128), lambda j: (1, 0, 0)),
            spec((None, None, 256, 128), lambda j: (1, 0, 0, 0)),
            spec((None, None, 256, 256), lambda j: (1, 0, 0, 0)),
        ],
        out_specs=[
            spec((CB, 128, 128), lambda j: (j, 0, 0)),
            spec((None, packed, 128), lambda j: (jnp.minimum(j, 2), 0, 0)),
            spec((None, packed, 128), lambda j: (0, 0, 0)),
            spec((2, 256, 128), lambda j: (0, 0, 0)),
        ],
        out_shape=[shape(NJ, 128, 128), shape(3, packed, 128), shape(1, packed, 128), shape(2, 256, 128)],
        compiler_params=PARAMS,
        cost_estimate=cost(1 << 30, 8 << 20),
        name="row_schur",
    )(basis0, cell_matrix, cell_list, cell_interp, cell_matrix)
    early_in = passed_along(early, "gx", -1)
    edge_in = passed_along(edge, "yz", -1)
    late_in = passed_along(late, "gx", -1)

    steps = NJ // CM
    lists = jnp.stack([cell_list, x_list, y_list]).reshape(3, 2, steps, CM, 128)
    lists = lists.transpose(2, 0, 1, 3, 4).reshape(steps, 6 * CM, 128)
    x_conduct = x_coupling[0].astype(F32).reshape(steps, CM, 128)
    y_conduct = y_coupling.astype(F32).reshape(2, steps, CM, 128)
    y_conduct = y_conduct.transpose(1, 0, 2, 3).reshape(steps, 2 * CM, 128)
    last = steps - 1
    x_face, y_face, bottom1, schur1, x_basis1 = pl.pallas_call(
        main_kernel,
        grid=(steps,),
        in_specs=[
            spec((None, 6 * CM, 128), lambda j: (last - j, 0, 0)),
            spec((CM, 128, 256), lambda j: (last - j, 0, 0)),
            spec((CM, 128, 128), lambda j: (last - j, 0, 0)),
            spec((None, CM, 256, 256), lambda j: (1, last - j, 0, 0)),
            spec((None, CM, 256, 128), lambda j: (1, last - j, 0, 0)),
            spec((2, CM, 256, 128), lambda j: (0, last - j, 0, 0)),
            spec((2, CM, 256, 128), lambda j: (0, last - j, 0, 0)),
            spec((None, CM, 128), lambda j: (last - j, 0, 0)),
            spec((None, 2 * CM, 128), lambda j: (last - j, 0, 0)),
        ],
        out_specs=[
            spec((None, CM, 128, 128), lambda j: (0, last - j, 0, 0)),
            spec((2, CM, 128, 128), lambda j: (0, last - j, 0, 0)),
            spec((CM, 128, 128), lambda j: (last - j, 0, 0)),
            spec((CM, 128, 128), lambda j: (last - j, 0, 0)),
            spec((CM, 128, 256), lambda j: (last - j, 0, 0)),
        ],
        out_shape=[
            shape(2, NJ, 128, 128),
            shape(2, NJ, 128, 128),
            shape(NJ, 128, 128),
            shape(NJ, 128, 128),
            shape(NJ, 128, 256),
        ],
        scratch_shapes=[pltpu.VMEM((2, 128, 128), BF16), pltpu.VMEM((2, 128, 128), BF16)],
        compiler_params=PARAMS,
        cost_estimate=cost(4 << 30, 30 << 20),
        name="main",
    )(lists, basis0, schur0, cell_matrix, cell_interp, x_face_interp, y_face_interp, x_conduct, y_conduct)

    end = NJ - 1
    edge_lists = jnp.pad(y_list[:, end], ((0, 6), (0, 0)))
    edge_conduct = jnp.pad(y_coupling[:, end].astype(F32), ((0, 6), (0, 0)))
    y_face = pl.pallas_call(
        edge_kernel,
        grid=(1,),
        in_specs=[
            spec((8, 128), lambda j: (0, 0)),
            spec((None, 128, 128), lambda j: (end, 0, 1)),
            spec((None, 128, 128), lambda j: (end, 0, 0)),
            spec((None, 128, 128), lambda j: (end, 0, 0)),
            spec((None, 128, 128), lambda j: (end, 0, 0)),
            spec((2, 256, 128), lambda j: (0, 0, 0)),
            spec((2, None, 256, 128), lambda j: (0, end, 0, 0)),
            spec((8, 128), lambda j: (0, 0)),
            pl.BlockSpec(memory_space=pl.ANY),
        ],
        out_specs=spec((2, None, 128, 128), lambda j: (0, end, 0, 0)),
        out_shape=shape(2, NJ, 128, 128),
        input_output_aliases={8: 0},
        compiler_params=PARAMS,
        cost_estimate=cost(1 << 27, 1 << 20),
        name="edge",
    )(edge_lists, basis0, bottom1, schur0, schur1, edge_in, y_face_interp, edge_conduct, y_face)

    x_conduct1 = x_coupling[1].astype(F32)
    for first, count, packed_in in ((0, 3, early_in), (3, 1, late_in)):
        x_face = pl.pallas_call(
            last_kernel,
            grid=(count,),
            in_specs=[
                spec((CB, 128, 128), lambda j, first=first: (first + j, 0, 0)),
                spec((CB, 128, 128), lambda j, first=first: (first + j, 0, 0)),
                spec((CB, 128, 256), lambda j, first=first: (first + j, 0, 0)),
                spec((CB, 128), lambda j, first=first: (first + j, 0)),
                spec((CB, 128, 128), lambda j, first=first: (first + j, 0, 0)),
                spec((None, packed, 128), lambda j: (j, 0, 0)),
                pl.BlockSpec(memory_space=pl.ANY),
            ],
            out_specs=spec((None, CB, 128, 128), lambda j, first=first: (1, first + j, 0, 0)),
            out_shape=shape(2, NJ, 128, 128),
            input_output_aliases={6: 0},
            compiler_params=PARAMS,
            cost_estimate=cost(count << 28, count << 21),
            name="last",
        )(bottom1, schur1, x_basis1, x_conduct1, top_in, packed_in, x_face)
    return x_face, y_face


def solution(mesh):
    cells, face, one = P("gx", "yz", None, None), P("gx", "yz", None), P("gx", "yz")
    return jax.shard_map(
        body,
        mesh=mesh,
        in_specs=(cells, face, face, cells, face, one, cells, face, one, cells, face, one),
        out_specs=(cells, cells),
        check_vma=False,
    )
```

```python
import jax
import jax.numpy as jnp
from jax import lax
from jax.experimental import pallas as pl
from jax.experimental.pallas import tpu as pltpu
from jax.sharding import PartitionSpec as P

F32, BF16 = jnp.float32, jnp.bfloat16
ROWS = (((1,), (1,)), ((), ()))
N = 16


def dot(a, b):
    return jnp.dot(a, b, preferred_element_type=F32).astype(BF16)


def dot_t(a, b):
    return lax.dot_general(a, b, ROWS, preferred_element_type=F32).astype(BF16)


def basis_of(skel, rank, interp, rows):
    one, zero = jnp.ones((), BF16), jnp.zeros((), BF16)
    slots = lax.broadcasted_iota(jnp.int32, (1, 128), 1)
    live = slots < rank
    marked = jnp.where(live, skel, -1).astype(F32).astype(BF16)
    picked = rows == jnp.broadcast_to(marked, (256, 128))
    kept = jnp.where(jnp.broadcast_to(live, (256, 128)), interp, zero)
    turned = jnp.where(picked, one, kept).T
    most = turned[:16]
    for k in range(1, 8):
        most = jnp.maximum(most, turned[16 * k : 16 * k + 16])
    most = jnp.max(most.astype(F32), axis=0, keepdims=True)
    least = jnp.where(most > 0.5, 0.5, -1.0).astype(BF16)
    return jnp.where(turned > jnp.broadcast_to(least, (128, 256)), turned, zero)


def mega(
    matrix_hbm, cell_hbm, x_hbm, y_hbm,
    x_conduct, y_conduct, cell_skel, x_skel, y_skel, cell_rank, x_rank, y_rank,
    x_out, y_out,
    matrix, interp, x_interp, y_interp, tops, bottoms, schurs, x_basis, basis, inner, face,
    x_face, y_face, packed, packed_in, diagonals, diagonals_in,
    in_sem, out_sem, send_sem, recv_sem,
):
    gx, yz = lax.axis_index("gx"), lax.axis_index("yz")
    gxs, yzs = lax.axis_size("gx"), lax.axis_size("yz")
    nj = cell_skel.shape[1]
    groups = nj // N
    has_down, has_up = gx > 0, gx < gxs - 1
    has_left, has_right = yz > 0, yz < yzs - 1

    copies = {}

    def load(name, src, dst):
        copies[name] = pltpu.make_async_copy(src, dst, in_sem.at[len(copies)])
        copies[name].start()

    span = [pl.ds(g * N, N) for g in range(groups)]
    for g in range(groups):
        load(("c", 0, g), cell_hbm.at[0, span[g]], interp.at[0, span[g]])
    for g in range(groups):
        load(("m", 0, g), matrix_hbm.at[0, span[g]], matrix.at[0, span[g]])
    for g in range(groups):
        load(("c", 1, g), cell_hbm.at[1, span[g]], interp.at[1, span[g]])
        load(("m", 1, g), matrix_hbm.at[1, span[g]], matrix.at[1, span[g]])
    for g in range(groups):
        load(("x", 0, g), x_hbm.at[0, span[g]], x_interp.at[0, span[g]])
    for g in range(groups):
        for row in range(2):
            load(("y", row, g), y_hbm.at[row, span[g]], y_interp.at[row, span[g]])
    for g in range(groups):
        load(("x", 1, g), x_hbm.at[1, span[g]], x_interp.at[1, span[g]])

    barrier = pltpu.get_barrier_semaphore()
    for there, device in (
        (has_down, {"gx": gx - 1}),
        (has_up, {"gx": gx + 1}),
        (has_left, {"yz": yz - 1}),
        (has_right, {"yz": yz + 1}),
    ):

        @pl.when(there)
        def _(device=device):
            pl.semaphore_signal(barrier, inc=1, device_id=device, device_id_type=pl.DeviceIdType.MESH)

    unknowns = lax.broadcasted_iota(jnp.int32, (256, 128), 0).astype(F32).astype(BF16)
    down = lax.broadcasted_iota(jnp.int32, (128, 128), 0)
    across = lax.broadcasted_iota(jnp.int32, (128, 128), 1)

    def remote(src, dst, at, device):
        return pltpu.make_async_remote_copy(
            src_ref=src, dst_ref=dst, send_sem=send_sem.at[at], recv_sem=recv_sem.at[at],
            device_id=device, device_id_type=pl.DeviceIdType.MESH,
        )

    top_copy = [
        remote(tops.at[0, span[g]], tops.at[2, span[g]], g, {"gx": gx - 1}) for g in range(groups)
    ]
    half = N // 2
    pack_copy = [
        remote(packed.at[pl.ds(g * half, half)], packed_in.at[pl.ds(g * half, half)], groups + g, {"gx": gx - 1})
        for g in range(groups)
    ]
    line_copy = [remote(diagonals.at[g], diagonals_in.at[g], 2 * groups + g, {"gx": gx - 1}) for g in range(groups)]
    side_copy = [
        remote(ref.at[pl.ds(0, 2), 0], ref.at[pl.ds(0, 2), nj], 3 * groups + k, {"yz": yz - 1})
        for k, ref in enumerate((tops, schurs))
    ]

    def cell_bases(row, g):
        for c in range(N):
            j = g * N + c
            value = basis_of(cell_skel[row, j : j + 1], cell_rank[row, j], interp[row, j], unknowns)
            tops[row, j] = value[:, :128]
            bottoms[row, j] = value[:, 128:]
            basis[c] = value

    def cell_schurs(row, g):
        for c in range(N):
            inner[c] = dot(basis[c], matrix[row, g * N + c])
        for c in range(N):
            schurs[row, g * N + c] = dot_t(inner[c], basis[c])

    def reload(row, g):
        for c in range(N):
            basis[c, :, :128] = tops[row, g * N + c]
            basis[c, :, 128:] = bottoms[row, g * N + c]

    def pack(g):
        lines = []
        for c in range(half):
            j = g * N + 2 * c
            packed[g * half + c] = jnp.where(down <= across, schurs[0, j], schurs[0, j + 1])
            lines.append(
                jnp.sum(jnp.where(down == across, schurs[0, j + 1].astype(F32), 0.0), axis=0, keepdims=True)
            )
        lines.append(jnp.zeros((16 - half, 128), F32))
        diagonals[g] = jnp.concatenate(lines, axis=0).astype(BF16)

    def unpack(g):
        for c in range(half):
            j = g * N + 2 * c
            value = packed_in[g * half + c]
            turned = value.T
            line = jnp.broadcast_to(diagonals_in[g, c : c + 1], (128, 128))
            schurs[2, j] = jnp.where(down <= across, value, turned)
            schurs[2, j + 1] = jnp.where(down == across, line, jnp.where(down > across, value, turned))

    def face_links(row, g, conduct, right):
        for c in range(N):
            j = g * N + c
            scaled = (tops[right(j)].astype(F32) * -conduct[row, j : j + 1].astype(F32)).astype(BF16)
            link = dot_t(bottoms[row, j], scaled)
            face[c, :128, :128] = schurs[row, j]
            face[c, :128, 128:] = link
            face[c, 128:, :128] = link.T

    def face_bases(row, g, skel, rank, values, into, base=0):
        for c in range(N):
            j = g * N + c
            into[base + c] = basis_of(skel[row, j : j + 1], rank[row, j], values[row, j], unknowns)

    def face_ends(row, g, right, bases, out, base=0):
        for c in range(N):
            face[c, 128:, 128:] = schurs[right(g * N + c)]
        for c in range(N):
            inner[c] = dot(bases[base + c], face[c])
        for c in range(N):
            out[row, g * N + c] = dot_t(bases[base + c], inner[c])

    outs = []

    def store(out, hbm, row, g):
        copy = pltpu.make_async_copy(out.at[row, span[g]], hbm.at[row, span[g]], out_sem.at[len(outs)])
        copy.start()
        outs.append(copy)

    count = sum(x.astype(jnp.int32) for x in (has_down, has_up, has_left, has_right))
    for g in range(groups):
        copies["c", 0, g].wait()
        cell_bases(0, g)
        if g == 0:
            pl.semaphore_wait(barrier, count)
        pl.when(has_down)(top_copy[g].start)
    for g in range(groups):
        reload(0, g)
        copies["m", 0, g].wait()
        cell_schurs(0, g)
        pack(g)
        pl.when(has_down)(pack_copy[g].start)
        pl.when(has_down)(line_copy[g].start)
    for g in range(groups):
        copies["c", 1, g].wait()
        cell_bases(1, g)
        copies["m", 1, g].wait()
        cell_schurs(1, g)
        if g == 0:
            for copy in side_copy:
                pl.when(has_left)(copy.start)

    @pl.when(jnp.logical_not(has_right))
    def _():
        for row in range(2):
            tops[row, nj] = jnp.zeros((128, 128), BF16)
            schurs[row, nj] = jnp.zeros((128, 128), BF16)

    @pl.when(jnp.logical_not(has_up))
    def _():
        tops[2] = jnp.zeros(tops.shape[1:], BF16)
        packed_in[...] = jnp.zeros_like(packed_in)
        diagonals_in[...] = jnp.zeros_like(diagonals_in)

    for g in range(groups):
        copies["x", 0, g].wait()
        face_links(0, g, x_conduct, lambda j: (1, j))
        face_bases(0, g, x_skel, x_rank, x_interp, basis)
        face_ends(0, g, lambda j: (1, j), basis, x_face)
        store(x_face, x_out, 0, g)
    for g in range(groups):
        if g == groups - 1:
            for copy in side_copy:
                pl.when(has_right)(copy.wait_recv)
        for row in range(2):
            copies["y", row, g].wait()
            face_links(row, g, y_conduct, lambda j, row=row: (row, j + 1))
            face_bases(row, g, y_skel, y_rank, y_interp, basis)
            face_ends(row, g, lambda j, row=row: (row, j + 1), basis, y_face)
            store(y_face, y_out, row, g)
    for g in range(groups):
        copies["x", 1, g].wait()
        face_bases(1, g, x_skel, x_rank, x_interp, x_basis, g * N)
    for g in range(groups):
        pl.when(has_up)(top_copy[g].wait_recv)
        face_links(1, g, x_conduct, lambda j: (2, j))
        pl.when(has_up)(pack_copy[g].wait_recv)
        pl.when(has_up)(line_copy[g].wait_recv)
        unpack(g)
        face_ends(1, g, lambda j: (2, j), x_basis, x_face, g * N)
        store(x_face, x_out, 1, g)
    for copy in outs:
        copy.wait()
    for copy in top_copy + pack_copy + line_copy:
        pl.when(has_down)(copy.wait_send)
    for copy in side_copy:
        pl.when(has_left)(copy.wait_send)


def body(*args):
    (
        cell_matrix, x_coupling, y_coupling, cell_interp, cell_skel, cell_rank,
        x_face_interp, x_face_skel, x_face_rank, y_face_interp, y_face_skel, y_face_rank,
    ) = args
    nj = cell_skel.shape[1]
    groups = nj // N
    hbm = pl.BlockSpec(memory_space=pl.ANY)
    vmem = pl.BlockSpec(memory_space=pltpu.VMEM)
    smem = pl.BlockSpec(memory_space=pltpu.SMEM)
    out = jax.ShapeDtypeStruct((2, nj, 128, 128), BF16)
    return pl.pallas_call(
        mega,
        in_specs=[hbm] * 4 + [vmem] * 5 + [smem] * 3,
        out_specs=[hbm] * 2,
        out_shape=[out] * 2,
        scratch_shapes=[
            pltpu.VMEM((2, nj, 256, 256), BF16),
            pltpu.VMEM((2, nj, 256, 128), BF16),
            pltpu.VMEM((2, nj, 256, 128), BF16),
            pltpu.VMEM((2, nj, 256, 128), BF16),
            pltpu.VMEM((3, nj + 1, 128, 128), BF16),
            pltpu.VMEM((2, nj, 128, 128), BF16),
            pltpu.VMEM((3, nj + 1, 128, 128), BF16),
            pltpu.VMEM((nj, 128, 256), BF16),
            pltpu.VMEM((N, 128, 256), BF16),
            pltpu.VMEM((N, 128, 256), BF16),
            pltpu.VMEM((N, 256, 256), BF16),
            pltpu.VMEM((2, nj, 128, 128), BF16),
            pltpu.VMEM((2, nj, 128, 128), BF16),
            pltpu.VMEM((nj // 2, 128, 128), BF16),
            pltpu.VMEM((nj // 2, 128, 128), BF16),
            pltpu.VMEM((groups, 16, 128), BF16),
            pltpu.VMEM((groups, 16, 128), BF16),
            pltpu.SemaphoreType.DMA((10 * groups,)),
            pltpu.SemaphoreType.DMA((4 * groups,)),
            pltpu.SemaphoreType.DMA((3 * groups + 2,)),
            pltpu.SemaphoreType.DMA((3 * groups + 2,)),
        ],
        compiler_params=pltpu.CompilerParams(
            collective_id=0, has_side_effects=True, vmem_limit_bytes=60 << 20
        ),
        name="mega",
    )(
        cell_matrix, cell_interp, x_face_interp, y_face_interp,
        x_coupling, y_coupling, cell_skel, x_face_skel, y_face_skel,
        cell_rank, x_face_rank, y_face_rank,
    )


def solution(mesh):
    cells, face, one = P("gx", "yz", None, None), P("gx", "yz", None), P("gx", "yz")
    return jax.shard_map(
        body,
        mesh=mesh,
        in_specs=(cells, face, face, cells, face, one, cells, face, one, cells, face, one),
        out_specs=(cells, cells),
        check_vma=False,
    )
```

```python
import jax
import jax.numpy as jnp
from jax import lax
from jax.experimental import pallas as pl
from jax.experimental.pallas import tpu as pltpu
from jax.sharding import PartitionSpec as P

F32, BF16 = jnp.float32, jnp.bfloat16
ROWS = (((1,), (1,)), ((), ()))
N = 16
CUTS = (0, 10, 18, 26, 32)


def dot(a, b):
    return jnp.dot(a, b, preferred_element_type=F32)


def dot_t(a, b):
    return lax.dot_general(a, b, ROWS, preferred_element_type=F32)


def basis_of(skel, rank, interp, rows):
    one, zero = jnp.ones((), BF16), jnp.zeros((), BF16)
    slots = lax.broadcasted_iota(jnp.int32, (1, 128), 1)
    live = slots < rank
    marked = jnp.where(live, skel, -1).astype(F32).astype(BF16)
    picked = rows == jnp.broadcast_to(marked, (256, 128))
    kept = jnp.where(jnp.broadcast_to(live, (256, 128)), interp, zero)
    turned = jnp.where(picked, one, kept).T
    most = turned[:16]
    for k in range(1, 8):
        most = jnp.maximum(most, turned[16 * k : 16 * k + 16])
    most = jnp.max(most.astype(F32), axis=0, keepdims=True)
    least = jnp.where(most > 0.5, 0.5, -1.0).astype(BF16)
    return jnp.where(turned > jnp.broadcast_to(least, (128, 256)), turned, zero)


def mega(
    matrix_hbm, cell_hbm, x_hbm, y_hbm,
    x_conduct, y_conduct, cell_skel, x_skel, y_skel, cell_rank, x_rank, y_rank,
    x_out, y_out,
    matrix, interp, x_interp, y_interp, tops, bottoms, schurs, x_basis, basis, inner, face,
    x_face, y_face, packed, packed_in, diagonals, diagonals_in, lifted, lifted_in, partial,
    in_sem, out_sem, send_sem, recv_sem,
):
    gx, yz = lax.axis_index("gx"), lax.axis_index("yz")
    gxs, yzs = lax.axis_size("gx"), lax.axis_size("yz")
    nj = cell_skel.shape[1]
    has_down, has_up = gx > 0, gx < gxs - 1
    has_left, has_right = yz > 0, yz < yzs - 1

    ranges = [range(*CUTS[k : k + 2]) for k in range(len(CUTS) - 1)]
    lower, upper = ranges[:2], ranges[2:]
    low = range(lower[0].start, lower[-1].stop)
    high = range(upper[0].start, upper[-1].stop)
    halves = [range(k, k + N) for k in range(0, nj, N)]

    def cut(cols):
        return pl.ds(cols.start, len(cols))

    copies = {}

    def load(kind, row, cols):
        src, dst = {
            "m": (matrix_hbm, matrix), "c": (cell_hbm, interp), "x": (x_hbm, x_interp), "y": (y_hbm, y_interp)
        }[kind]
        copy = pltpu.make_async_copy(src.at[row, cut(cols)], dst.at[row, cut(cols)], in_sem.at[len(copies)])
        copy.start()
        copies[kind, row, cols] = copy

    def loaded(kind, row, cols):
        copies[kind, row, cols].wait()

    for k in range(2):
        load("c", 0, lower[k])
        load("c", 1, upper[k])
        load("x", 1, upper[k])
    load("m", 0, low)
    load("c", 0, high)
    load("m", 0, high)
    load("c", 1, low)
    load("m", 1, low)
    load("m", 1, high)
    for cols in halves:
        load("x", 0, cols)
    for cols in halves:
        load("y", 0, cols)
        load("y", 1, cols)
    load("x", 1, low)

    barrier = pltpu.get_barrier_semaphore()
    for there, device in (
        (has_down, {"gx": gx - 1}),
        (has_up, {"gx": gx + 1}),
        (has_left, {"yz": yz - 1}),
        (has_right, {"yz": yz + 1}),
    ):

        @pl.when(there)
        def _(device=device):
            pl.semaphore_signal(barrier, inc=1, device_id=device, device_id_type=pl.DeviceIdType.MESH)

    unknowns = lax.broadcasted_iota(jnp.int32, (256, 128), 0).astype(F32).astype(BF16)
    down = lax.broadcasted_iota(jnp.int32, (128, 128), 0)
    across = lax.broadcasted_iota(jnp.int32, (128, 128), 1)

    made = []

    def remote(src, dst, device):
        at = len(made)
        made.append(at)
        return pltpu.make_async_remote_copy(
            src_ref=src, dst_ref=dst, send_sem=send_sem.at[at], recv_sem=recv_sem.at[at],
            device_id=device, device_id_type=pl.DeviceIdType.MESH,
        )

    lift = [
        remote(lifted.at[part], lifted_in.at[part], {"gx": gx + 1})
        for part in (pl.ds(cols.start - high.start, len(cols)) for cols in upper)
    ]
    top_copy = [remote(tops.at[0, cut(cols)], tops.at[2, cut(cols)], {"gx": gx - 1}) for cols in lower]
    pack_copy = []
    for k, cols in enumerate(ranges):
        pairs = pl.ds(cols.start // 2, len(cols) // 2)
        pack_copy.append(
            (
                remote(packed.at[pairs], packed_in.at[pairs], {"gx": gx - 1}),
                remote(diagonals.at[k], diagonals_in.at[k], {"gx": gx - 1}),
            )
        )
    side_copy = [
        remote(ref.at[pl.ds(0, 2), 0], ref.at[pl.ds(0, 2), nj], {"yz": yz - 1}) for ref in (tops, schurs)
    ]

    outs = []

    def store(kind, row, cols):
        src, dst = {"x": (x_face, x_out), "y": (y_face, y_out)}[kind]
        copy = pltpu.make_async_copy(src.at[row, cut(cols)], dst.at[row, cut(cols)], out_sem.at[len(outs)])
        copy.start()
        outs.append(copy)

    def cell(row, j):
        return jnp.concatenate([tops[row, j], bottoms[row, j]], axis=1)

    def cell_bases(row, cols):
        for j in cols:
            value = basis_of(cell_skel[row, j : j + 1], cell_rank[row, j], interp[row, j], unknowns)
            tops[row, j] = value[:, :128]
            bottoms[row, j] = value[:, 128:]

    def cell_schurs(row, cols):
        for c, j in enumerate(cols):
            inner[c] = dot(cell(row, j), matrix[row, j]).astype(BF16)
        for c, j in enumerate(cols):
            schurs[row, j] = dot_t(inner[c], cell(row, j)).astype(BF16)

    def pack(k, blocks):
        lines = []
        for c, j in enumerate(range(ranges[k].start, ranges[k].stop, 2)):
            packed[j // 2] = jnp.where(down <= across, blocks(j), blocks(j + 1))
            lines.append(jnp.sum(jnp.where(down == across, blocks(j + 1).astype(F32), 0.0), axis=0, keepdims=True))
        lines.append(jnp.zeros((16 - len(lines), 128), F32))
        diagonals[k] = jnp.concatenate(lines, axis=0).astype(BF16)

    def unpack(k):
        for c, j in enumerate(range(ranges[k].start, ranges[k].stop, 2)):
            value = packed_in[j // 2]
            turned = value.T
            line = jnp.broadcast_to(diagonals_in[k, c : c + 1], (128, 128))
            schurs[2, j] = jnp.where(down <= across, value, turned)
            schurs[2, j + 1] = jnp.where(down == across, line, jnp.where(down > across, value, turned))

    def face_bases(row, cols, skel, rank, values, into):
        for c, j in enumerate(cols):
            into[c] = basis_of(skel[row, j : j + 1], rank[row, j], values[row, j], unknowns)

    def negative(conduct, row, j):
        return -conduct[row, j : j + 1].astype(F32)

    def face_links(row, cols, conduct, right):
        for c, j in enumerate(cols):
            scaled = (tops[right(j)].astype(F32) * negative(conduct, row, j)).astype(BF16)
            link = dot_t(bottoms[row, j], scaled).astype(BF16)
            face[c, :128, :128] = schurs[row, j]
            face[c, :128, 128:] = link
            face[c, 128:, :128] = link.T

    def face_ends(row, cols, right, bases, out, base=0):
        for c, j in enumerate(cols):
            face[base + c, 128:, 128:] = schurs[right(j)]
        for c, j in enumerate(cols):
            inner[c] = dot(bases[base + c], face[base + c]).astype(BF16)
        for c, j in enumerate(cols):
            out[row, j] = dot_t(bases[base + c], inner[c]).astype(BF16)

    def lift_out(cols):
        for j in cols:
            value = basis_of(x_skel[1, j : j + 1], x_rank[1, j], x_interp[1, j], unknowns)
            x_basis[j] = value
            lifted[j - high.start, :, :128] = value[:, 128:]
        for j in cols:
            carried = dot(x_basis[j, :, :128], bottoms[1, j]) * negative(x_conduct, 1, j)
            lifted[j - high.start, :, 128:] = carried.astype(BF16)

    def lift_back(cols):
        for c, j in enumerate(cols):
            both = jnp.concatenate([schurs[0, j], tops[0, j]], axis=1)
            inner[c] = dot(lifted_in[j - high.start, :, :128], both).astype(BF16)
        for c, j in enumerate(cols):
            here = lifted_in[j - high.start]
            value = dot_t(here, inner[c]) + dot_t(inner[c, :, 128:], here[:, 128:])
            face[c, :128, :128] = value.astype(BF16)

    def own_part(cols):
        for c, j in enumerate(cols):
            inner[c, :, :128] = dot(x_basis[j, :, :128], schurs[1, j]).astype(BF16)
        for c, j in enumerate(cols):
            partial[j - high.start] = dot_t(x_basis[j, :, :128], inner[c, :, :128])

    def send(k):
        for copy in pack_copy[k]:
            pl.when(has_down)(copy.start)

    def received(k):
        for copy in pack_copy[k]:
            pl.when(has_up)(copy.wait_recv)

    count = sum(x.astype(jnp.int32) for x in (has_down, has_up, has_left, has_right))
    for k in range(2):
        loaded("c", 0, lower[k])
        cell_bases(0, lower[k])
        if k == 0:
            pl.semaphore_wait(barrier, count)
        pl.when(has_down)(top_copy[k].start)
        loaded("c", 1, upper[k])
        loaded("x", 1, upper[k])
        cell_bases(1, upper[k])
        lift_out(upper[k])
        pl.when(has_up)(lift[k].start)
    loaded("m", 0, low)
    cell_schurs(0, low)
    for k in range(2):
        pack(k, lambda j: schurs[0, j])
        send(k)
    loaded("c", 0, high)
    cell_bases(0, high)
    loaded("m", 0, high)
    cell_schurs(0, high)
    loaded("c", 1, low)
    cell_bases(1, low)
    loaded("m", 1, low)
    cell_schurs(1, low)
    for copy in side_copy:
        pl.when(has_left)(copy.start)
    loaded("m", 1, high)
    cell_schurs(1, high)

    @pl.when(jnp.logical_not(has_right))
    def _():
        for row in range(2):
            tops[row, nj] = jnp.zeros((128, 128), BF16)
            schurs[row, nj] = jnp.zeros((128, 128), BF16)

    @pl.when(jnp.logical_not(has_up))
    def _():
        tops[2] = jnp.zeros(tops.shape[1:], BF16)
        packed_in[...] = jnp.zeros_like(packed_in)
        diagonals_in[...] = jnp.zeros_like(diagonals_in)

    def own_faces(row, cols, kind):
        loaded(kind, row, cols)
        if kind == "x":
            right = lambda j: (1, j)
            face_links(row, cols, x_conduct, right)
            face_bases(row, cols, x_skel, x_rank, x_interp, basis)
            face_ends(row, cols, right, basis, x_face)
        else:
            right = lambda j: (row, j + 1)
            face_links(row, cols, y_conduct, right)
            face_bases(row, cols, y_skel, y_rank, y_interp, basis)
            face_ends(row, cols, right, basis, y_face)
        store(kind, row, cols)

    def answer(k):
        @pl.when(has_down)
        def _():
            lift[k].wait_recv()
            cols = upper[k]
            lift_back(cols)
            pack(2 + k, lambda j: face[j - cols.start, :128, :128])
            for copy in pack_copy[2 + k]:
                copy.start()

    for cols in halves:
        own_faces(0, cols, "x")
    own_faces(0, halves[0], "y")
    own_faces(1, halves[0], "y")
    answer(0)
    for copy in side_copy:
        pl.when(has_right)(copy.wait_recv)
    own_faces(0, halves[1], "y")
    own_faces(1, halves[1], "y")
    own_part(high)
    answer(1)
    loaded("x", 1, low)
    face_bases(1, low, x_skel, x_rank, x_interp, x_basis)
    for copy in top_copy:
        pl.when(has_up)(copy.wait_recv)
    face_links(1, low, x_conduct, lambda j: (2, j))
    for k in range(2):
        received(k)
        unpack(k)
        face_ends(1, lower[k], lambda j: (2, j), x_basis, x_face, lower[k].start)
        store("x", 1, lower[k])
    for k in range(2):
        received(2 + k)
        unpack(2 + k)
        for j in upper[k]:
            x_face[1, j] = (partial[j - high.start] + schurs[2, j].astype(F32)).astype(BF16)
        store("x", 1, upper[k])
    for copy in outs:
        copy.wait()
    for copy in top_copy + [copy for pair in pack_copy for copy in pair]:
        pl.when(has_down)(copy.wait_send)
    for copy in lift:
        pl.when(has_up)(copy.wait_send)
    for copy in side_copy:
        pl.when(has_left)(copy.wait_send)


def finish(x_in, y_in, x_out, y_out, held, in_sem, out_sem):
    rows, columns = x_in.shape[:2]
    pieces = [
        (src.at[row, part], held.at[k, row, part], dst.at[row, part])
        for k, (src, dst) in enumerate(((x_in, x_out), (y_in, y_out)))
        for row in range(rows)
        for part in (pl.ds(at, N) for at in range(0, columns, N))
    ]
    arrive = [pltpu.make_async_copy(src, here, in_sem.at[k]) for k, (src, here, _) in enumerate(pieces)]
    leave = [pltpu.make_async_copy(here, dst, out_sem.at[k]) for k, (_, here, dst) in enumerate(pieces)]
    for copy in arrive:
        copy.start()
    for before, after in zip(arrive, leave):
        before.wait()
        after.start()
    for copy in leave:
        copy.wait()


def body(*args):
    (
        cell_matrix, x_coupling, y_coupling, cell_interp, cell_skel, cell_rank,
        x_face_interp, x_face_skel, x_face_rank, y_face_interp, y_face_skel, y_face_rank,
    ) = args
    nj = cell_skel.shape[1]
    high, most = CUTS[-1] - CUTS[2], max(N, CUTS[2], CUTS[-1] - CUTS[2])
    hbm = pl.BlockSpec(memory_space=pl.ANY)
    vmem = pl.BlockSpec(memory_space=pltpu.VMEM)
    smem = pl.BlockSpec(memory_space=pltpu.SMEM)
    out = jax.ShapeDtypeStruct((2, nj, 128, 128), BF16)
    faces = pl.pallas_call(
        mega,
        in_specs=[hbm] * 4 + [vmem] * 5 + [smem] * 3,
        out_specs=[hbm] * 2,
        out_shape=[out] * 2,
        scratch_shapes=[
            pltpu.VMEM((2, nj, 256, 256), BF16),
            pltpu.VMEM((2, nj, 256, 128), BF16),
            pltpu.VMEM((2, nj, 256, 128), BF16),
            pltpu.VMEM((2, nj, 256, 128), BF16),
            pltpu.VMEM((3, nj + 1, 128, 128), BF16),
            pltpu.VMEM((2, nj, 128, 128), BF16),
            pltpu.VMEM((3, nj + 1, 128, 128), BF16),
            pltpu.VMEM((nj, 128, 256), BF16),
            pltpu.VMEM((N, 128, 256), BF16),
            pltpu.VMEM((most, 128, 256), BF16),
            pltpu.VMEM((most, 256, 256), BF16),
            pltpu.VMEM((2, nj, 128, 128), BF16),
            pltpu.VMEM((2, nj, 128, 128), BF16),
            pltpu.VMEM((nj // 2, 128, 128), BF16),
            pltpu.VMEM((nj // 2, 128, 128), BF16),
            pltpu.VMEM((4, 16, 128), BF16),
            pltpu.VMEM((4, 16, 128), BF16),
            pltpu.VMEM((high, 128, 256), BF16),
            pltpu.VMEM((high, 128, 256), BF16),
            pltpu.VMEM((high, 128, 128), F32),
            pltpu.SemaphoreType.DMA((19,)),
            pltpu.SemaphoreType.DMA((10,)),
            pltpu.SemaphoreType.DMA((14,)),
            pltpu.SemaphoreType.DMA((14,)),
        ],
        compiler_params=pltpu.CompilerParams(
            collective_id=0, has_side_effects=True, vmem_limit_bytes=60 << 20
        ),
        name="mega",
    )(
        cell_matrix, cell_interp, x_face_interp, y_face_interp,
        x_coupling, y_coupling, cell_skel, x_face_skel, y_face_skel,
        cell_rank, x_face_rank, y_face_rank,
    )
    return pl.pallas_call(
        finish,
        in_specs=[hbm] * 2,
        out_specs=[hbm] * 2,
        out_shape=[out] * 2,
        scratch_shapes=[
            pltpu.VMEM((2, 2, nj, 128, 128), BF16),
            pltpu.SemaphoreType.DMA((4 * nj // N,)),
            pltpu.SemaphoreType.DMA((4 * nj // N,)),
        ],
        compiler_params=pltpu.CompilerParams(vmem_limit_bytes=60 << 20),
        name="finish",
    )(*faces)


def solution(mesh):
    cells, face, one = P("gx", "yz", None, None), P("gx", "yz", None), P("gx", "yz")
    return jax.shard_map(
        body,
        mesh=mesh,
        in_specs=(cells, face, face, cells, face, one, cells, face, one, cells, face, one),
        out_specs=(cells, cells),
        check_vma=False,
    )
```

```python
import jax
import jax.numpy as jnp
from jax import lax
from jax.experimental import pallas as pl
from jax.experimental.pallas import tpu as pltpu
from jax.sharding import PartitionSpec as P

F32, BF16 = jnp.float32, jnp.bfloat16
ROWS = (((1,), (1,)), ((), ()))
N = 16
LOWER = ((0, 6), (6, 18))
UPPER = ((18, 22), (22, 28), (28, 32))


def dot(a, b):
    return jnp.dot(a, b, preferred_element_type=F32)


def dot_t(a, b):
    return lax.dot_general(a, b, ROWS, preferred_element_type=F32)


def basis_of(skel, rank, interp, rows):
    one, zero = jnp.ones((), BF16), jnp.zeros((), BF16)
    slots = lax.broadcasted_iota(jnp.int32, (1, 128), 1)
    live = slots < rank
    marked = jnp.where(live, skel, -1).astype(F32).astype(BF16)
    picked = rows == jnp.broadcast_to(marked, (256, 128))
    kept = jnp.where(jnp.broadcast_to(live, (256, 128)), interp, zero)
    turned = jnp.where(picked, one, kept).T
    most = turned[:16]
    for k in range(1, 8):
        most = jnp.maximum(most, turned[16 * k : 16 * k + 16])
    most = jnp.max(most.astype(F32), axis=0, keepdims=True)
    least = jnp.where(most > 0.5, 0.5, -1.0).astype(BF16)
    return jnp.where(turned > jnp.broadcast_to(least, (128, 256)), turned, zero)


def mega(
    matrix_hbm, cell_hbm, x_hbm, y_hbm,
    x_conduct, y_conduct, cell_skel, x_skel, y_skel, cell_rank, x_rank, y_rank,
    x_out, y_out,
    matrix, interp, x_interp, y_interp, tops, bottoms, schurs, x_basis, basis, inner, face,
    x_face, y_face, packed, packed_in, diagonals, diagonals_in, lifted, lifted_in, partial,
    in_sem, out_sem, send_sem, recv_sem,
):
    gx, yz = lax.axis_index("gx"), lax.axis_index("yz")
    gxs, yzs = lax.axis_size("gx"), lax.axis_size("yz")
    nj = cell_skel.shape[1]
    has_down, has_up = gx > 0, gx < gxs - 1
    has_left, has_right = yz > 0, yz < yzs - 1

    lower, upper = [range(*ends) for ends in LOWER], [range(*ends) for ends in UPPER]
    ranges = lower + upper
    low = range(lower[0].start, lower[-1].stop)
    high = range(upper[0].start, upper[-1].stop)
    halves = [range(k, k + N) for k in range(0, nj, N)]

    def cut(cols):
        return pl.ds(cols.start, len(cols))

    copies = {}

    def load(kind, row, cols):
        src, dst = {
            "m": (matrix_hbm, matrix), "c": (cell_hbm, interp), "x": (x_hbm, x_interp), "y": (y_hbm, y_interp)
        }[kind]
        copy = pltpu.make_async_copy(src.at[row, cut(cols)], dst.at[row, cut(cols)], in_sem.at[len(copies)])
        copy.start()
        copies[kind, row, cols] = copy

    def loaded(kind, row, cols):
        copies[kind, row, cols].wait()

    for k, cols in enumerate(upper):
        load("c", 1, cols)
        load("x", 1, cols)
        if k < len(lower):
            load("c", 0, lower[k])
    load("m", 0, low)
    load("c", 0, high)
    load("m", 0, high)
    load("c", 1, low)
    load("m", 1, low)
    load("m", 1, high)
    for cols in halves:
        load("x", 0, cols)
    for cols in halves:
        load("y", 0, cols)
        load("y", 1, cols)
    load("x", 1, low)

    barrier = pltpu.get_barrier_semaphore()
    for there, device in (
        (has_down, {"gx": gx - 1}),
        (has_up, {"gx": gx + 1}),
        (has_left, {"yz": yz - 1}),
        (has_right, {"yz": yz + 1}),
    ):

        @pl.when(there)
        def _(device=device):
            pl.semaphore_signal(barrier, inc=1, device_id=device, device_id_type=pl.DeviceIdType.MESH)

    unknowns = lax.broadcasted_iota(jnp.int32, (256, 128), 0).astype(F32).astype(BF16)
    down = lax.broadcasted_iota(jnp.int32, (128, 128), 0)
    across = lax.broadcasted_iota(jnp.int32, (128, 128), 1)

    made = []

    def remote(src, dst, device):
        at = len(made)
        made.append(at)
        return pltpu.make_async_remote_copy(
            src_ref=src, dst_ref=dst, send_sem=send_sem.at[at], recv_sem=recv_sem.at[at],
            device_id=device, device_id_type=pl.DeviceIdType.MESH,
        )

    lift = [
        remote(lifted.at[part], lifted_in.at[part], {"gx": gx + 1})
        for part in (pl.ds(cols.start - high.start, len(cols)) for cols in upper)
    ]
    top_copy = [remote(tops.at[0, cut(cols)], tops.at[2, cut(cols)], {"gx": gx - 1}) for cols in lower]
    pack_copy = []
    for k, cols in enumerate(ranges):
        pairs = pl.ds(cols.start // 2, len(cols) // 2)
        pack_copy.append(
            (
                remote(packed.at[pairs], packed_in.at[pairs], {"gx": gx - 1}),
                remote(diagonals.at[k], diagonals_in.at[k], {"gx": gx - 1}),
            )
        )
    side_copy = [
        remote(ref.at[pl.ds(0, 2), 0], ref.at[pl.ds(0, 2), nj], {"yz": yz - 1}) for ref in (tops, schurs)
    ]

    outs = []

    def store(kind, row, cols):
        src, dst = {"x": (x_face, x_out), "y": (y_face, y_out)}[kind]
        copy = pltpu.make_async_copy(src.at[row, cut(cols)], dst.at[row, cut(cols)], out_sem.at[len(outs)])
        copy.start()
        outs.append(copy)

    def cell(row, j):
        return jnp.concatenate([tops[row, j], bottoms[row, j]], axis=1)

    def cell_bases(row, cols):
        for j in cols:
            value = basis_of(cell_skel[row, j : j + 1], cell_rank[row, j], interp[row, j], unknowns)
            tops[row, j] = value[:, :128]
            bottoms[row, j] = value[:, 128:]

    def cell_schurs(row, cols):
        for c, j in enumerate(cols):
            inner[c] = dot(cell(row, j), matrix[row, j]).astype(BF16)
        for c, j in enumerate(cols):
            schurs[row, j] = dot_t(inner[c], cell(row, j)).astype(BF16)

    def pack(k, blocks):
        lines = []
        for c, j in enumerate(range(ranges[k].start, ranges[k].stop, 2)):
            packed[j // 2] = jnp.where(down <= across, blocks(j), blocks(j + 1))
            lines.append(jnp.sum(jnp.where(down == across, blocks(j + 1).astype(F32), 0.0), axis=0, keepdims=True))
        lines.append(jnp.zeros((16 - len(lines), 128), F32))
        diagonals[k] = jnp.concatenate(lines, axis=0).astype(BF16)

    def unpack(k):
        for c, j in enumerate(range(ranges[k].start, ranges[k].stop, 2)):
            value = packed_in[j // 2]
            turned = value.T
            line = jnp.broadcast_to(diagonals_in[k, c : c + 1], (128, 128))
            schurs[2, j] = jnp.where(down <= across, value, turned)
            schurs[2, j + 1] = jnp.where(down == across, line, jnp.where(down > across, value, turned))

    def face_bases(row, cols, skel, rank, values, into):
        for c, j in enumerate(cols):
            into[c] = basis_of(skel[row, j : j + 1], rank[row, j], values[row, j], unknowns)

    def negative(conduct, row, j):
        return -conduct[row, j : j + 1].astype(F32)

    def face_links(row, cols, conduct, right):
        for c, j in enumerate(cols):
            scaled = (tops[right(j)].astype(F32) * negative(conduct, row, j)).astype(BF16)
            link = dot_t(bottoms[row, j], scaled).astype(BF16)
            face[c, :128, :128] = schurs[row, j]
            face[c, :128, 128:] = link
            face[c, 128:, :128] = link.T

    def face_ends(row, cols, right, bases, out, base=0):
        for c, j in enumerate(cols):
            face[base + c, 128:, 128:] = schurs[right(j)]
        for c, j in enumerate(cols):
            inner[c] = dot(bases[base + c], face[base + c]).astype(BF16)
        for c, j in enumerate(cols):
            out[row, j] = dot_t(bases[base + c], inner[c]).astype(BF16)

    def lift_out(cols):
        for j in cols:
            value = basis_of(x_skel[1, j : j + 1], x_rank[1, j], x_interp[1, j], unknowns)
            x_basis[j] = value
            lifted[j - high.start, :, :128] = value[:, 128:]
        for j in cols:
            carried = dot(x_basis[j, :, :128], bottoms[1, j]) * negative(x_conduct, 1, j)
            lifted[j - high.start, :, 128:] = carried.astype(BF16)

    def lift_back(cols):
        for c, j in enumerate(cols):
            both = jnp.concatenate([schurs[0, j], tops[0, j]], axis=1)
            inner[c] = dot(lifted_in[j - high.start, :, :128], both).astype(BF16)
        for c, j in enumerate(cols):
            here = lifted_in[j - high.start]
            value = dot_t(here, inner[c]) + dot_t(inner[c, :, 128:], here[:, 128:])
            face[c, :128, :128] = value.astype(BF16)

    def own_part(cols):
        for c, j in enumerate(cols):
            inner[c, :, :128] = dot(x_basis[j, :, :128], schurs[1, j]).astype(BF16)
        for c, j in enumerate(cols):
            partial[j - high.start] = dot_t(x_basis[j, :, :128], inner[c, :, :128])

    def send(k):
        for copy in pack_copy[k]:
            pl.when(has_down)(copy.start)

    def received(k):
        for copy in pack_copy[k]:
            pl.when(has_up)(copy.wait_recv)

    count = sum(x.astype(jnp.int32) for x in (has_down, has_up, has_left, has_right))
    for k, cols in enumerate(upper):
        loaded("c", 1, cols)
        loaded("x", 1, cols)
        cell_bases(1, cols)
        lift_out(cols)
        if k == 0:
            pl.semaphore_wait(barrier, count)
        pl.when(has_up)(lift[k].start)
        if k < len(lower):
            loaded("c", 0, lower[k])
            cell_bases(0, lower[k])
            pl.when(has_down)(top_copy[k].start)
    loaded("m", 0, low)
    cell_schurs(0, low)
    for k in range(len(lower)):
        pack(k, lambda j: schurs[0, j])
        send(k)
    loaded("c", 0, high)
    cell_bases(0, high)
    loaded("m", 0, high)
    cell_schurs(0, high)
    loaded("c", 1, low)
    cell_bases(1, low)
    loaded("m", 1, low)
    cell_schurs(1, low)
    for copy in side_copy:
        pl.when(has_left)(copy.start)
    loaded("m", 1, high)
    cell_schurs(1, high)

    @pl.when(jnp.logical_not(has_right))
    def _():
        for row in range(2):
            tops[row, nj] = jnp.zeros((128, 128), BF16)
            schurs[row, nj] = jnp.zeros((128, 128), BF16)

    @pl.when(jnp.logical_not(has_up))
    def _():
        tops[2] = jnp.zeros(tops.shape[1:], BF16)
        packed_in[...] = jnp.zeros_like(packed_in)
        diagonals_in[...] = jnp.zeros_like(diagonals_in)

    def own_faces(row, cols, kind):
        loaded(kind, row, cols)
        if kind == "x":
            right = lambda j: (1, j)
            face_links(row, cols, x_conduct, right)
            face_bases(row, cols, x_skel, x_rank, x_interp, basis)
            face_ends(row, cols, right, basis, x_face)
        else:
            right = lambda j: (row, j + 1)
            face_links(row, cols, y_conduct, right)
            face_bases(row, cols, y_skel, y_rank, y_interp, basis)
            face_ends(row, cols, right, basis, y_face)
        store(kind, row, cols)

    def answer(k):
        @pl.when(has_down)
        def _():
            lift[k].wait_recv()
            cols = upper[k]
            lift_back(cols)
            pack(len(lower) + k, lambda j: face[j - cols.start, :128, :128])
            for copy in pack_copy[len(lower) + k]:
                copy.start()

    for cols in halves:
        own_faces(0, cols, "x")
    own_faces(0, halves[0], "y")
    own_faces(1, halves[0], "y")
    answer(0)
    for copy in side_copy:
        pl.when(has_right)(copy.wait_recv)
    own_faces(0, halves[1], "y")
    own_faces(1, halves[1], "y")
    answer(1)
    own_part(high)
    loaded("x", 1, low)
    face_bases(1, low, x_skel, x_rank, x_interp, x_basis)
    for copy in top_copy:
        pl.when(has_up)(copy.wait_recv)
    face_links(1, low, x_conduct, lambda j: (2, j))
    for k, cols in enumerate(lower):
        received(k)
        unpack(k)
        face_ends(1, cols, lambda j: (2, j), x_basis, x_face, cols.start)
        store("x", 1, cols)
    answer(2)
    for k, cols in enumerate(upper, len(lower)):
        received(k)
        unpack(k)
        for j in cols:
            x_face[1, j] = (partial[j - high.start] + schurs[2, j].astype(F32)).astype(BF16)
        store("x", 1, cols)
    for copy in outs:
        copy.wait()
    for copy in top_copy + [copy for pair in pack_copy for copy in pair]:
        pl.when(has_down)(copy.wait_send)
    for copy in lift:
        pl.when(has_up)(copy.wait_send)
    for copy in side_copy:
        pl.when(has_left)(copy.wait_send)


def finish(x_in, y_in, x_out, y_out, held, in_sem, out_sem):
    pieces = [
        (src.at[row], held.at[k, row], dst.at[row])
        for k, (src, dst) in enumerate(((x_in, x_out), (y_in, y_out)))
        for row in range(x_in.shape[0])
    ]
    arrive = [pltpu.make_async_copy(src, here, in_sem.at[k]) for k, (src, here, _) in enumerate(pieces)]
    leave = [pltpu.make_async_copy(here, dst, out_sem.at[k]) for k, (_, here, dst) in enumerate(pieces)]
    for copy in arrive:
        copy.start()
    for before, after in zip(arrive, leave):
        before.wait()
        after.start()
    for copy in leave:
        copy.wait()


def body(*args):
    (
        cell_matrix, x_coupling, y_coupling, cell_interp, cell_skel, cell_rank,
        x_face_interp, x_face_skel, x_face_rank, y_face_interp, y_face_skel, y_face_rank,
    ) = args
    nj = cell_skel.shape[1]
    low, high = LOWER[-1][1] - LOWER[0][0], UPPER[-1][1] - UPPER[0][0]
    most = max(N, low, high)
    hbm = pl.BlockSpec(memory_space=pl.ANY)
    vmem = pl.BlockSpec(memory_space=pltpu.VMEM)
    smem = pl.BlockSpec(memory_space=pltpu.SMEM)
    out = jax.ShapeDtypeStruct((2, nj, 128, 128), BF16)
    faces = pl.pallas_call(
        mega,
        in_specs=[hbm] * 4 + [vmem] * 5 + [smem] * 3,
        out_specs=[hbm] * 2,
        out_shape=[out] * 2,
        scratch_shapes=[
            pltpu.VMEM((2, nj, 256, 256), BF16),
            pltpu.VMEM((2, nj, 256, 128), BF16),
            pltpu.VMEM((2, nj, 256, 128), BF16),
            pltpu.VMEM((2, nj, 256, 128), BF16),
            pltpu.VMEM((3, nj + 1, 128, 128), BF16),
            pltpu.VMEM((2, nj, 128, 128), BF16),
            pltpu.VMEM((3, nj + 1, 128, 128), BF16),
            pltpu.VMEM((nj, 128, 256), BF16),
            pltpu.VMEM((N, 128, 256), BF16),
            pltpu.VMEM((most, 128, 256), BF16),
            pltpu.VMEM((most, 256, 256), BF16),
            pltpu.VMEM((2, nj, 128, 128), BF16),
            pltpu.VMEM((2, nj, 128, 128), BF16),
            pltpu.VMEM((nj // 2, 128, 128), BF16),
            pltpu.VMEM((nj // 2, 128, 128), BF16),
            pltpu.VMEM((len(LOWER + UPPER), 16, 128), BF16),
            pltpu.VMEM((len(LOWER + UPPER), 16, 128), BF16),
            pltpu.VMEM((high, 128, 256), BF16),
            pltpu.VMEM((high, 128, 256), BF16),
            pltpu.VMEM((high, 128, 128), F32),
            pltpu.SemaphoreType.DMA((21,)),
            pltpu.SemaphoreType.DMA((11,)),
            pltpu.SemaphoreType.DMA((17,)),
            pltpu.SemaphoreType.DMA((17,)),
        ],
        compiler_params=pltpu.CompilerParams(
            collective_id=0, has_side_effects=True, vmem_limit_bytes=60 << 20
        ),
        name="mega",
    )(
        cell_matrix, cell_interp, x_face_interp, y_face_interp,
        x_coupling, y_coupling, cell_skel, x_face_skel, y_face_skel,
        cell_rank, x_face_rank, y_face_rank,
    )
    return pl.pallas_call(
        finish,
        in_specs=[hbm] * 2,
        out_specs=[hbm] * 2,
        out_shape=[out] * 2,
        scratch_shapes=[
            pltpu.VMEM((2, 2, nj, 128, 128), BF16),
            pltpu.SemaphoreType.DMA((4,)),
            pltpu.SemaphoreType.DMA((4,)),
        ],
        compiler_params=pltpu.CompilerParams(vmem_limit_bytes=60 << 20),
        name="finish",
    )(*faces)


def solution(mesh):
    cells, face, one = P("gx", "yz", None, None), P("gx", "yz", None), P("gx", "yz")
    return jax.shard_map(
        body,
        mesh=mesh,
        in_specs=(cells, face, face, cells, face, one, cells, face, one, cells, face, one),
        out_specs=(cells, cells),
        check_vma=False,
    )
```

```python
import jax
import jax.numpy as jnp
from jax import lax
from jax.experimental import pallas as pl
from jax.experimental.pallas import tpu as pltpu
from jax.sharding import PartitionSpec as P

F32, BF16 = jnp.float32, jnp.bfloat16
ROWS = (((1,), (1,)), ((), ()))
N = 16
LOWER = ((0, 4), (4, 18))
UPPER = ((18, 22), (22, 28), (28, 32))


def dot(a, b):
    return jnp.dot(a, b, preferred_element_type=F32)


def dot_t(a, b):
    return lax.dot_general(a, b, ROWS, preferred_element_type=F32)


def basis_of(skel, rank, interp, rows):
    one, zero = jnp.ones((), BF16), jnp.zeros((), BF16)
    slots = lax.broadcasted_iota(jnp.int32, (1, 128), 1)
    live = slots < rank
    marked = jnp.where(live, skel, -1).astype(F32).astype(BF16)
    picked = rows == jnp.broadcast_to(marked, (256, 128))
    kept = jnp.where(jnp.broadcast_to(live, (256, 128)), interp, zero)
    turned = jnp.where(picked, one, kept).T
    most = turned[:16]
    for k in range(1, 8):
        most = jnp.maximum(most, turned[16 * k : 16 * k + 16])
    most = jnp.max(most.astype(F32), axis=0, keepdims=True)
    least = jnp.where(most > 0.5, 0.5, -1.0).astype(BF16)
    return jnp.where(turned > jnp.broadcast_to(least, (128, 256)), turned, zero)


def mega(
    matrix_hbm, cell_hbm, x_hbm, y_hbm,
    x_conduct, y_conduct, cell_skel, x_skel, y_skel, cell_rank, x_rank, y_rank,
    x_out, y_out,
    matrix, interp, x_interp, y_interp, tops, bottoms, schurs, x_basis, basis, inner, face,
    x_face, y_face, packed, packed_in, diagonals, diagonals_in, lifted, lifted_in, partial,
    in_sem, out_sem, send_sem, recv_sem,
):
    gx, yz = lax.axis_index("gx"), lax.axis_index("yz")
    gxs, yzs = lax.axis_size("gx"), lax.axis_size("yz")
    nj = cell_skel.shape[1]
    has_down, has_up = gx > 0, gx < gxs - 1
    has_left, has_right = yz > 0, yz < yzs - 1

    lower, upper = [range(*ends) for ends in LOWER], [range(*ends) for ends in UPPER]
    ranges = lower + upper
    low = range(lower[0].start, lower[-1].stop)
    high = range(upper[0].start, upper[-1].stop)
    halves = [range(k, k + N) for k in range(0, nj, N)]

    def cut(cols):
        return pl.ds(cols.start, len(cols))

    copies = {}

    def load(kind, row, cols):
        src, dst = {
            "m": (matrix_hbm, matrix), "c": (cell_hbm, interp), "x": (x_hbm, x_interp), "y": (y_hbm, y_interp)
        }[kind]
        copy = pltpu.make_async_copy(src.at[row, cut(cols)], dst.at[row, cut(cols)], in_sem.at[len(copies)])
        copy.start()
        copies[kind, row, cols] = copy

    def loaded(kind, row, cols):
        copies[kind, row, cols].wait()

    for k, cols in enumerate(upper):
        if k < len(lower):
            load("c", 0, lower[k])
        load("c", 1, cols)
        load("x", 1, cols)
    load("m", 0, low)
    load("c", 0, high)
    load("m", 0, high)
    load("c", 1, low)
    load("m", 1, low)
    load("m", 1, high)
    for cols in halves:
        load("x", 0, cols)
    for cols in halves:
        load("y", 0, cols)
        load("y", 1, cols)
    load("x", 1, low)

    barrier = pltpu.get_barrier_semaphore()
    for there, device in (
        (has_down, {"gx": gx - 1}),
        (has_up, {"gx": gx + 1}),
        (has_left, {"yz": yz - 1}),
        (has_right, {"yz": yz + 1}),
    ):

        @pl.when(there)
        def _(device=device):
            pl.semaphore_signal(barrier, inc=1, device_id=device, device_id_type=pl.DeviceIdType.MESH)

    unknowns = lax.broadcasted_iota(jnp.int32, (256, 128), 0).astype(F32).astype(BF16)
    down = lax.broadcasted_iota(jnp.int32, (128, 128), 0)
    across = lax.broadcasted_iota(jnp.int32, (128, 128), 1)

    made = []

    def remote(src, dst, device):
        at = len(made)
        made.append(at)
        return pltpu.make_async_remote_copy(
            src_ref=src, dst_ref=dst, send_sem=send_sem.at[at], recv_sem=recv_sem.at[at],
            device_id=device, device_id_type=pl.DeviceIdType.MESH,
        )

    lift = [
        remote(lifted.at[part], lifted_in.at[part], {"gx": gx + 1})
        for part in (pl.ds(cols.start - high.start, len(cols)) for cols in upper)
    ]
    top_copy = [remote(tops.at[0, cut(cols)], tops.at[2, cut(cols)], {"gx": gx - 1}) for cols in lower]
    pack_copy = []
    for k, cols in enumerate(ranges):
        pairs = pl.ds(cols.start // 2, len(cols) // 2)
        pack_copy.append(
            (
                remote(packed.at[pairs], packed_in.at[pairs], {"gx": gx - 1}),
                remote(diagonals.at[k], diagonals_in.at[k], {"gx": gx - 1}),
            )
        )
    side_copy = [
        remote(ref.at[pl.ds(0, 2), 0], ref.at[pl.ds(0, 2), nj], {"yz": yz - 1}) for ref in (tops, schurs)
    ]

    outs = []

    def store(kind, row, cols):
        src, dst = {"x": (x_face, x_out), "y": (y_face, y_out)}[kind]
        copy = pltpu.make_async_copy(src.at[row, cut(cols)], dst.at[row, cut(cols)], out_sem.at[len(outs)])
        copy.start()
        outs.append(copy)

    def cell(row, j):
        return jnp.concatenate([tops[row, j], bottoms[row, j]], axis=1)

    def cell_bases(row, cols):
        for j in cols:
            value = basis_of(cell_skel[row, j : j + 1], cell_rank[row, j], interp[row, j], unknowns)
            tops[row, j] = value[:, :128]
            bottoms[row, j] = value[:, 128:]

    def cell_schurs(row, cols):
        for c, j in enumerate(cols):
            inner[c] = dot(cell(row, j), matrix[row, j]).astype(BF16)
        for c, j in enumerate(cols):
            schurs[row, j] = dot_t(inner[c], cell(row, j)).astype(BF16)

    def pack(k, blocks):
        lines = []
        for c, j in enumerate(range(ranges[k].start, ranges[k].stop, 2)):
            packed[j // 2] = jnp.where(down <= across, blocks(j), blocks(j + 1))
            lines.append(jnp.sum(jnp.where(down == across, blocks(j + 1).astype(F32), 0.0), axis=0, keepdims=True))
        lines.append(jnp.zeros((16 - len(lines), 128), F32))
        diagonals[k] = jnp.concatenate(lines, axis=0).astype(BF16)

    def unpack(k):
        for c, j in enumerate(range(ranges[k].start, ranges[k].stop, 2)):
            value = packed_in[j // 2]
            turned = value.T
            line = jnp.broadcast_to(diagonals_in[k, c : c + 1], (128, 128))
            schurs[2, j] = jnp.where(down <= across, value, turned)
            schurs[2, j + 1] = jnp.where(down == across, line, jnp.where(down > across, value, turned))

    def face_bases(row, cols, skel, rank, values, into):
        for c, j in enumerate(cols):
            into[c] = basis_of(skel[row, j : j + 1], rank[row, j], values[row, j], unknowns)

    def negative(conduct, row, j):
        return -conduct[row, j : j + 1].astype(F32)

    def face_links(row, cols, conduct, right):
        for c, j in enumerate(cols):
            scaled = (tops[right(j)].astype(F32) * negative(conduct, row, j)).astype(BF16)
            link = dot_t(bottoms[row, j], scaled).astype(BF16)
            face[c, :128, :128] = schurs[row, j]
            face[c, :128, 128:] = link
            face[c, 128:, :128] = link.T

    def face_ends(row, cols, right, bases, out, base=0):
        for c, j in enumerate(cols):
            face[base + c, 128:, 128:] = schurs[right(j)]
        for c, j in enumerate(cols):
            inner[c] = dot(bases[base + c], face[base + c]).astype(BF16)
        for c, j in enumerate(cols):
            out[row, j] = dot_t(bases[base + c], inner[c]).astype(BF16)

    def lift_out(cols):
        for j in cols:
            value = basis_of(x_skel[1, j : j + 1], x_rank[1, j], x_interp[1, j], unknowns)
            x_basis[j] = value
            lifted[j - high.start, :, :128] = value[:, 128:]
        for j in cols:
            carried = dot(x_basis[j, :, :128], bottoms[1, j]) * negative(x_conduct, 1, j)
            lifted[j - high.start, :, 128:] = carried.astype(BF16)

    def lift_back(cols):
        for c, j in enumerate(cols):
            both = jnp.concatenate([schurs[0, j], tops[0, j]], axis=1)
            inner[c] = dot(lifted_in[j - high.start, :, :128], both).astype(BF16)
        for c, j in enumerate(cols):
            here = lifted_in[j - high.start]
            value = dot_t(here, inner[c]) + dot_t(inner[c, :, 128:], here[:, 128:])
            face[c, :128, :128] = value.astype(BF16)

    def own_part(cols):
        for c, j in enumerate(cols):
            inner[c, :, :128] = dot(x_basis[j, :, :128], schurs[1, j]).astype(BF16)
        for c, j in enumerate(cols):
            partial[j - high.start] = dot_t(x_basis[j, :, :128], inner[c, :, :128])

    def send(k):
        for copy in pack_copy[k]:
            pl.when(has_down)(copy.start)

    def received(k):
        for copy in pack_copy[k]:
            pl.when(has_up)(copy.wait_recv)

    count = sum(x.astype(jnp.int32) for x in (has_down, has_up, has_left, has_right))
    for k, cols in enumerate(upper):
        if k < len(lower):
            loaded("c", 0, lower[k])
            cell_bases(0, lower[k])
            if k == 0:
                pl.semaphore_wait(barrier, count)
            pl.when(has_down)(top_copy[k].start)
        loaded("c", 1, cols)
        loaded("x", 1, cols)
        cell_bases(1, cols)
        lift_out(cols)
        pl.when(has_up)(lift[k].start)
    loaded("m", 0, low)
    cell_schurs(0, low)
    for k in range(len(lower)):
        pack(k, lambda j: schurs[0, j])
        send(k)
    loaded("c", 0, high)
    cell_bases(0, high)
    loaded("m", 0, high)
    cell_schurs(0, high)
    loaded("c", 1, low)
    cell_bases(1, low)
    loaded("m", 1, low)
    cell_schurs(1, low)
    for copy in side_copy:
        pl.when(has_left)(copy.start)
    loaded("m", 1, high)
    cell_schurs(1, high)

    @pl.when(jnp.logical_not(has_right))
    def _():
        for row in range(2):
            tops[row, nj] = jnp.zeros((128, 128), BF16)
            schurs[row, nj] = jnp.zeros((128, 128), BF16)

    @pl.when(jnp.logical_not(has_up))
    def _():
        tops[2] = jnp.zeros(tops.shape[1:], BF16)
        packed_in[...] = jnp.zeros_like(packed_in)
        diagonals_in[...] = jnp.zeros_like(diagonals_in)

    def own_faces(row, cols, kind):
        loaded(kind, row, cols)
        if kind == "x":
            right = lambda j: (1, j)
            face_links(row, cols, x_conduct, right)
            face_bases(row, cols, x_skel, x_rank, x_interp, basis)
            face_ends(row, cols, right, basis, x_face)
        else:
            right = lambda j: (row, j + 1)
            face_links(row, cols, y_conduct, right)
            face_bases(row, cols, y_skel, y_rank, y_interp, basis)
            face_ends(row, cols, right, basis, y_face)
        store(kind, row, cols)

    def answer(k):
        @pl.when(has_down)
        def _():
            lift[k].wait_recv()
            cols = upper[k]
            lift_back(cols)
            pack(len(lower) + k, lambda j: face[j - cols.start, :128, :128])
            for copy in pack_copy[len(lower) + k]:
                copy.start()

    for cols in halves:
        own_faces(0, cols, "x")
    own_faces(0, halves[0], "y")
    own_faces(1, halves[0], "y")
    answer(0)
    for copy in side_copy:
        pl.when(has_right)(copy.wait_recv)
    own_faces(0, halves[1], "y")
    own_faces(1, halves[1], "y")
    answer(1)
    own_part(high)
    loaded("x", 1, low)
    face_bases(1, low, x_skel, x_rank, x_interp, x_basis)
    for copy in top_copy:
        pl.when(has_up)(copy.wait_recv)
    face_links(1, low, x_conduct, lambda j: (2, j))
    for k, cols in enumerate(lower):
        received(k)
        unpack(k)
        face_ends(1, cols, lambda j: (2, j), x_basis, x_face, cols.start)
        store("x", 1, cols)
    answer(2)
    for k, cols in enumerate(upper, len(lower)):
        received(k)
        unpack(k)
        for j in cols:
            x_face[1, j] = (partial[j - high.start] + schurs[2, j].astype(F32)).astype(BF16)
        store("x", 1, cols)
    for copy in outs:
        copy.wait()
    for copy in top_copy + [copy for pair in pack_copy for copy in pair]:
        pl.when(has_down)(copy.wait_send)
    for copy in lift:
        pl.when(has_up)(copy.wait_send)
    for copy in side_copy:
        pl.when(has_left)(copy.wait_send)


def finish(x_in, y_in, x_out, y_out, held, in_sem, out_sem):
    pieces = [
        (src.at[row], held.at[k, row], dst.at[row])
        for k, (src, dst) in enumerate(((x_in, x_out), (y_in, y_out)))
        for row in range(x_in.shape[0])
    ]
    arrive = [pltpu.make_async_copy(src, here, in_sem.at[k]) for k, (src, here, _) in enumerate(pieces)]
    leave = [pltpu.make_async_copy(here, dst, out_sem.at[k]) for k, (_, here, dst) in enumerate(pieces)]
    for copy in arrive:
        copy.start()
    for before, after in zip(arrive, leave):
        before.wait()
        after.start()
    for copy in leave:
        copy.wait()


def body(*args):
    (
        cell_matrix, x_coupling, y_coupling, cell_interp, cell_skel, cell_rank,
        x_face_interp, x_face_skel, x_face_rank, y_face_interp, y_face_skel, y_face_rank,
    ) = args
    nj = cell_skel.shape[1]
    low, high = LOWER[-1][1] - LOWER[0][0], UPPER[-1][1] - UPPER[0][0]
    most = max(N, low, high)
    hbm = pl.BlockSpec(memory_space=pl.ANY)
    vmem = pl.BlockSpec(memory_space=pltpu.VMEM)
    smem = pl.BlockSpec(memory_space=pltpu.SMEM)
    out = jax.ShapeDtypeStruct((2, nj, 128, 128), BF16)
    faces = pl.pallas_call(
        mega,
        in_specs=[hbm] * 4 + [vmem] * 5 + [smem] * 3,
        out_specs=[hbm] * 2,
        out_shape=[out] * 2,
        scratch_shapes=[
            pltpu.VMEM((2, nj, 256, 256), BF16),
            pltpu.VMEM((2, nj, 256, 128), BF16),
            pltpu.VMEM((2, nj, 256, 128), BF16),
            pltpu.VMEM((2, nj, 256, 128), BF16),
            pltpu.VMEM((3, nj + 1, 128, 128), BF16),
            pltpu.VMEM((2, nj, 128, 128), BF16),
            pltpu.VMEM((3, nj + 1, 128, 128), BF16),
            pltpu.VMEM((nj, 128, 256), BF16),
            pltpu.VMEM((N, 128, 256), BF16),
            pltpu.VMEM((most, 128, 256), BF16),
            pltpu.VMEM((most, 256, 256), BF16),
            pltpu.VMEM((2, nj, 128, 128), BF16),
            pltpu.VMEM((2, nj, 128, 128), BF16),
            pltpu.VMEM((nj // 2, 128, 128), BF16),
            pltpu.VMEM((nj // 2, 128, 128), BF16),
            pltpu.VMEM((len(LOWER + UPPER), 16, 128), BF16),
            pltpu.VMEM((len(LOWER + UPPER), 16, 128), BF16),
            pltpu.VMEM((high, 128, 256), BF16),
            pltpu.VMEM((high, 128, 256), BF16),
            pltpu.VMEM((high, 128, 128), F32),
            pltpu.SemaphoreType.DMA((21,)),
            pltpu.SemaphoreType.DMA((11,)),
            pltpu.SemaphoreType.DMA((17,)),
            pltpu.SemaphoreType.DMA((17,)),
        ],
        compiler_params=pltpu.CompilerParams(
            collective_id=0, has_side_effects=True, vmem_limit_bytes=60 << 20
        ),
        name="mega",
    )(
        cell_matrix, cell_interp, x_face_interp, y_face_interp,
        x_coupling, y_coupling, cell_skel, x_face_skel, y_face_skel,
        cell_rank, x_face_rank, y_face_rank,
    )
    return pl.pallas_call(
        finish,
        in_specs=[hbm] * 2,
        out_specs=[hbm] * 2,
        out_shape=[out] * 2,
        scratch_shapes=[
            pltpu.VMEM((2, 2, nj, 128, 128), BF16),
            pltpu.SemaphoreType.DMA((4,)),
            pltpu.SemaphoreType.DMA((4,)),
        ],
        compiler_params=pltpu.CompilerParams(vmem_limit_bytes=60 << 20),
        name="finish",
    )(*faces)


def solution(mesh):
    cells, face, one = P("gx", "yz", None, None), P("gx", "yz", None), P("gx", "yz")
    return jax.shard_map(
        body,
        mesh=mesh,
        in_specs=(cells, face, face, cells, face, one, cells, face, one, cells, face, one),
        out_specs=(cells, cells),
        check_vma=False,
    )
```

```python
import jax
import jax.numpy as jnp
from jax import lax
from jax.experimental import pallas as pl
from jax.experimental.pallas import tpu as pltpu
from jax.sharding import PartitionSpec as P

F32, BF16 = jnp.float32, jnp.bfloat16
ROWS = (((1,), (1,)), ((), ()))
N = 16
LOWER = ((0, 4), (4, 18))
UPPER = ((18, 22), (22, 28), (28, 32))


def dot(a, b):
    return jnp.dot(a, b, preferred_element_type=F32)


def dot_t(a, b):
    return lax.dot_general(a, b, ROWS, preferred_element_type=F32)


def basis_of(skel, rank, interp, rows):
    one, zero = jnp.ones((), BF16), jnp.zeros((), BF16)
    slots = lax.broadcasted_iota(jnp.int32, (1, 128), 1)
    live = slots < rank
    marked = jnp.where(live, skel, -1).astype(F32).astype(BF16)
    picked = rows == jnp.broadcast_to(marked, (256, 128))
    kept = jnp.where(jnp.broadcast_to(live, (256, 128)), interp, zero)
    turned = jnp.where(picked, one, kept).T
    most = turned[:16]
    for k in range(1, 8):
        most = jnp.maximum(most, turned[16 * k : 16 * k + 16])
    most = jnp.max(most.astype(F32), axis=0, keepdims=True)
    least = jnp.where(most > 0.5, 0.5, -1.0).astype(BF16)
    return jnp.where(turned > jnp.broadcast_to(least, (128, 256)), turned, zero)


def mega(
    matrix_hbm, cell_hbm, x_hbm, y_hbm,
    x_conduct, y_conduct, cell_skel, x_skel, y_skel, cell_rank, x_rank, y_rank,
    x_out, y_out, late_packed, late_lines, late_part,
    matrix, interp, x_interp, y_interp, tops, bottoms, schurs, x_basis, basis, inner, face,
    x_face, y_face, packed, packed_in, diagonals, diagonals_in, lifted, lifted_in, partial,
    late_sem, in_sem, out_sem, send_sem, recv_sem,
):
    gx, yz = lax.axis_index("gx"), lax.axis_index("yz")
    gxs, yzs = lax.axis_size("gx"), lax.axis_size("yz")
    nj = cell_skel.shape[1]
    has_down, has_up = gx > 0, gx < gxs - 1
    has_left, has_right = yz > 0, yz < yzs - 1

    lower, upper = [range(*ends) for ends in LOWER], [range(*ends) for ends in UPPER]
    ranges = lower + upper
    low = range(lower[0].start, lower[-1].stop)
    high = range(upper[0].start, upper[-1].stop)
    halves = [range(k, k + N) for k in range(0, nj, N)]

    def cut(cols):
        return pl.ds(cols.start, len(cols))

    barrier = pltpu.get_barrier_semaphore()
    for there, device in (
        (has_down, {"gx": gx - 1}),
        (has_up, {"gx": gx + 1}),
        (has_left, {"yz": yz - 1}),
        (has_right, {"yz": yz + 1}),
    ):

        @pl.when(there)
        def _(device=device):
            pl.semaphore_signal(barrier, inc=1, device_id=device, device_id_type=pl.DeviceIdType.MESH)

    copies = {}

    def load(kind, row, cols):
        src, dst = {
            "m": (matrix_hbm, matrix), "c": (cell_hbm, interp), "x": (x_hbm, x_interp), "y": (y_hbm, y_interp)
        }[kind]
        copy = pltpu.make_async_copy(src.at[row, cut(cols)], dst.at[row, cut(cols)], in_sem.at[len(copies)])
        copy.start()
        copies[kind, row, cols] = copy

    def loaded(kind, row, cols):
        copies[kind, row, cols].wait()

    for k, cols in enumerate(upper):
        if k < len(lower):
            load("c", 0, lower[k])
        load("c", 1, cols)
        load("x", 1, cols)
    load("m", 0, low)
    load("c", 0, high)
    load("m", 0, high)
    load("c", 1, low)
    load("m", 1, low)
    load("m", 1, high)
    for cols in halves:
        load("x", 0, cols)
    for cols in halves:
        load("y", 0, cols)
        load("y", 1, cols)
    load("x", 1, low)

    unknowns = lax.broadcasted_iota(jnp.int32, (256, 128), 0).astype(F32).astype(BF16)
    down = lax.broadcasted_iota(jnp.int32, (128, 128), 0)
    across = lax.broadcasted_iota(jnp.int32, (128, 128), 1)

    made = []

    def remote(src, dst, device):
        at = len(made)
        made.append(at)
        return pltpu.make_async_remote_copy(
            src_ref=src, dst_ref=dst, send_sem=send_sem.at[at], recv_sem=recv_sem.at[at],
            device_id=device, device_id_type=pl.DeviceIdType.MESH,
        )

    lift = [
        remote(lifted.at[part], lifted_in.at[part], {"gx": gx + 1})
        for part in (pl.ds(cols.start - high.start, len(cols)) for cols in upper)
    ]
    top_copy = [remote(tops.at[0, cut(cols)], tops.at[2, cut(cols)], {"gx": gx - 1}) for cols in lower]
    pack_copy = []
    for k, cols in enumerate(ranges):
        pairs = pl.ds(cols.start // 2, len(cols) // 2)
        late = cols is upper[-1]
        pack_copy.append(
            (
                remote(packed.at[pairs], late_packed if late else packed_in.at[pairs], {"gx": gx - 1}),
                remote(diagonals.at[k], late_lines if late else diagonals_in.at[k], {"gx": gx - 1}),
            )
        )
    side_copy = [
        remote(ref.at[pl.ds(0, 2), 0], ref.at[pl.ds(0, 2), nj], {"yz": yz - 1}) for ref in (tops, schurs)
    ]

    outs = []

    def store(kind, row, cols):
        src, dst = {"x": (x_face, x_out), "y": (y_face, y_out)}[kind]
        copy = pltpu.make_async_copy(src.at[row, cut(cols)], dst.at[row, cut(cols)], out_sem.at[len(outs)])
        copy.start()
        outs.append(copy)

    def cell(row, j):
        return jnp.concatenate([tops[row, j], bottoms[row, j]], axis=1)

    def cell_bases(row, cols):
        for j in cols:
            value = basis_of(cell_skel[row, j : j + 1], cell_rank[row, j], interp[row, j], unknowns)
            tops[row, j] = value[:, :128]
            bottoms[row, j] = value[:, 128:]

    def cell_schurs(row, cols):
        for c, j in enumerate(cols):
            inner[c] = dot(cell(row, j), matrix[row, j]).astype(BF16)
        for c, j in enumerate(cols):
            schurs[row, j] = dot_t(inner[c], cell(row, j)).astype(BF16)

    def pack(k, blocks):
        lines = []
        for c, j in enumerate(range(ranges[k].start, ranges[k].stop, 2)):
            packed[j // 2] = jnp.where(down <= across, blocks(j), blocks(j + 1))
            lines.append(jnp.sum(jnp.where(down == across, blocks(j + 1).astype(F32), 0.0), axis=0, keepdims=True))
        lines.append(jnp.zeros((16 - len(lines), 128), F32))
        diagonals[k] = jnp.concatenate(lines, axis=0).astype(BF16)

    def unpack(k):
        for c, j in enumerate(range(ranges[k].start, ranges[k].stop, 2)):
            value = packed_in[j // 2]
            turned = value.T
            line = jnp.broadcast_to(diagonals_in[k, c : c + 1], (128, 128))
            schurs[2, j] = jnp.where(down <= across, value, turned)
            schurs[2, j + 1] = jnp.where(down == across, line, jnp.where(down > across, value, turned))

    def face_bases(row, cols, skel, rank, values, into):
        for c, j in enumerate(cols):
            into[c] = basis_of(skel[row, j : j + 1], rank[row, j], values[row, j], unknowns)

    def negative(conduct, row, j):
        return -conduct[row, j : j + 1].astype(F32)

    def face_links(row, cols, conduct, right):
        for c, j in enumerate(cols):
            scaled = (tops[right(j)].astype(F32) * negative(conduct, row, j)).astype(BF16)
            link = dot_t(bottoms[row, j], scaled).astype(BF16)
            face[c, :128, :128] = schurs[row, j]
            face[c, :128, 128:] = link
            face[c, 128:, :128] = link.T

    def face_ends(row, cols, right, bases, out, base=0):
        for c, j in enumerate(cols):
            face[base + c, 128:, 128:] = schurs[right(j)]
        for c, j in enumerate(cols):
            inner[c] = dot(bases[base + c], face[base + c]).astype(BF16)
        for c, j in enumerate(cols):
            out[row, j] = dot_t(bases[base + c], inner[c]).astype(BF16)

    def lift_out(cols):
        for j in cols:
            value = basis_of(x_skel[1, j : j + 1], x_rank[1, j], x_interp[1, j], unknowns)
            x_basis[j] = value
            lifted[j - high.start, :, :128] = value[:, 128:]
        for j in cols:
            carried = dot(x_basis[j, :, :128], bottoms[1, j]) * negative(x_conduct, 1, j)
            lifted[j - high.start, :, 128:] = carried.astype(BF16)

    def lift_back(cols):
        for c, j in enumerate(cols):
            both = jnp.concatenate([schurs[0, j], tops[0, j]], axis=1)
            inner[c] = dot(lifted_in[j - high.start, :, :128], both).astype(BF16)
        for c, j in enumerate(cols):
            here = lifted_in[j - high.start]
            value = dot_t(here, inner[c]) + dot_t(inner[c, :, 128:], here[:, 128:])
            face[c, :128, :128] = value.astype(BF16)

    def own_part(cols):
        for c, j in enumerate(cols):
            inner[c, :, :128] = dot(x_basis[j, :, :128], schurs[1, j]).astype(BF16)
        for c, j in enumerate(cols):
            partial[j - high.start] = dot_t(x_basis[j, :, :128], inner[c, :, :128])

    def send(k):
        for copy in pack_copy[k]:
            pl.when(has_down)(copy.start)

    def received(k):
        for copy in pack_copy[k]:
            pl.when(has_up)(copy.wait_recv)

    count = sum(x.astype(jnp.int32) for x in (has_down, has_up, has_left, has_right))
    for k, cols in enumerate(upper):
        if k < len(lower):
            loaded("c", 0, lower[k])
            cell_bases(0, lower[k])
            if k == 0:
                pl.semaphore_wait(barrier, count)
            pl.when(has_down)(top_copy[k].start)
        loaded("c", 1, cols)
        loaded("x", 1, cols)
        cell_bases(1, cols)
        lift_out(cols)
        pl.when(has_up)(lift[k].start)
    loaded("m", 0, low)
    cell_schurs(0, low)
    for k in range(len(lower)):
        pack(k, lambda j: schurs[0, j])
        send(k)
    loaded("c", 0, high)
    cell_bases(0, high)
    loaded("m", 0, high)
    cell_schurs(0, high)
    loaded("c", 1, low)
    cell_bases(1, low)
    loaded("m", 1, low)
    cell_schurs(1, low)
    for copy in side_copy:
        pl.when(has_left)(copy.start)
    loaded("m", 1, high)
    cell_schurs(1, high)

    @pl.when(jnp.logical_not(has_right))
    def _():
        for row in range(2):
            tops[row, nj] = jnp.zeros((128, 128), BF16)
            schurs[row, nj] = jnp.zeros((128, 128), BF16)

    @pl.when(jnp.logical_not(has_up))
    def _():
        tops[2] = jnp.zeros(tops.shape[1:], BF16)
        packed_in[...] = jnp.zeros_like(packed_in)
        diagonals_in[...] = jnp.zeros_like(diagonals_in)

    def own_faces(row, cols, kind):
        loaded(kind, row, cols)
        if kind == "x":
            right = lambda j: (1, j)
            face_links(row, cols, x_conduct, right)
            face_bases(row, cols, x_skel, x_rank, x_interp, basis)
            face_ends(row, cols, right, basis, x_face)
        else:
            right = lambda j: (row, j + 1)
            face_links(row, cols, y_conduct, right)
            face_bases(row, cols, y_skel, y_rank, y_interp, basis)
            face_ends(row, cols, right, basis, y_face)
        store(kind, row, cols)

    def answer(k):
        @pl.when(has_down)
        def _():
            lift[k].wait_recv()
            cols = upper[k]
            lift_back(cols)
            pack(len(lower) + k, lambda j: face[j - cols.start, :128, :128])
            for copy in pack_copy[len(lower) + k]:
                copy.start()

    for cols in halves:
        own_faces(0, cols, "x")
    own_faces(0, halves[0], "y")
    own_faces(1, halves[0], "y")
    answer(0)
    for copy in side_copy:
        pl.when(has_right)(copy.wait_recv)
    own_faces(0, halves[1], "y")
    own_faces(1, halves[1], "y")
    answer(1)
    own_part(high)
    loaded("x", 1, low)
    face_bases(1, low, x_skel, x_rank, x_interp, x_basis)
    for copy in top_copy:
        pl.when(has_up)(copy.wait_recv)
    face_links(1, low, x_conduct, lambda j: (2, j))
    last = pl.ds(upper[-1].start - high.start, len(upper[-1]))
    part_copy = pltpu.make_async_copy(partial.at[last], late_part, late_sem.at[0])
    part_copy.start()
    fill = [
        pltpu.make_async_copy(packed_in.at[pl.ds(0, len(upper[-1]) // 2)], late_packed, late_sem.at[1]),
        pltpu.make_async_copy(diagonals_in.at[0], late_lines, late_sem.at[2]),
    ]

    @pl.when(jnp.logical_not(has_up))
    def _():
        for copy in fill:
            copy.start()
        for copy in fill:
            copy.wait()

    for k, cols in enumerate(lower):
        if k == len(lower) - 1:
            answer(len(upper) - 1)
        received(k)
        unpack(k)
        face_ends(1, cols, lambda j: (2, j), x_basis, x_face, cols.start)
        store("x", 1, cols)
    for k, cols in enumerate(upper[:-1], len(lower)):
        received(k)
        unpack(k)
        for j in cols:
            x_face[1, j] = (partial[j - high.start] + schurs[2, j].astype(F32)).astype(BF16)
        store("x", 1, cols)
    part_copy.wait()
    received(len(ranges) - 1)
    for copy in outs:
        copy.wait()
    for copy in top_copy + [copy for pair in pack_copy for copy in pair]:
        pl.when(has_down)(copy.wait_send)
    for copy in lift:
        pl.when(has_up)(copy.wait_send)
    for copy in side_copy:
        pl.when(has_left)(copy.wait_send)


def finish(x_in, y_in, packed_in, lines_in, part_in, x_out, y_out, held, packed, lines, part, in_sem, out_sem):
    first, stop = UPPER[-1]
    early, late = pl.ds(0, first), pl.ds(first, stop - first)
    pieces = [
        (y_in.at[0], held.at[1, 0], y_out.at[0]),
        (y_in.at[1], held.at[1, 1], y_out.at[1]),
        (x_in.at[0], held.at[0, 0], x_out.at[0]),
        (x_in.at[1, early], held.at[0, 1, early], x_out.at[1, early]),
    ]
    arrive = [pltpu.make_async_copy(src, here, in_sem.at[k]) for k, (src, here, _) in enumerate(pieces)]
    leave = [pltpu.make_async_copy(here, dst, out_sem.at[k]) for k, (_, here, dst) in enumerate(pieces)]
    for src, here in ((packed_in, packed), (lines_in, lines), (part_in, part)):
        arrive.append(pltpu.make_async_copy(src, here, in_sem.at[len(arrive)]))
    for copy in arrive:
        copy.start()
    for before, after in zip(arrive, leave):
        before.wait()
        after.start()
    for copy in arrive[len(leave) :]:
        copy.wait()
    down = lax.broadcasted_iota(jnp.int32, (128, 128), 0)
    across = lax.broadcasted_iota(jnp.int32, (128, 128), 1)
    for c in range((stop - first) // 2):
        value = packed[c]
        turned = value.T
        line = jnp.broadcast_to(lines[c : c + 1], (128, 128))
        one = jnp.where(down <= across, value, turned)
        two = jnp.where(down == across, line, jnp.where(down > across, value, turned))
        for k, answer in ((2 * c, one), (2 * c + 1, two)):
            held[0, 1, first + k] = (part[k] + answer.astype(F32)).astype(BF16)
    leave.append(pltpu.make_async_copy(held.at[0, 1, late], x_out.at[1, late], out_sem.at[len(leave)]))
    leave[-1].start()
    for copy in leave:
        copy.wait()


def body(*args):
    (
        cell_matrix, x_coupling, y_coupling, cell_interp, cell_skel, cell_rank,
        x_face_interp, x_face_skel, x_face_rank, y_face_interp, y_face_skel, y_face_rank,
    ) = args
    nj = cell_skel.shape[1]
    low, high = LOWER[-1][1] - LOWER[0][0], UPPER[-1][1] - UPPER[0][0]
    most = max(N, low, high)
    hbm = pl.BlockSpec(memory_space=pl.ANY)
    vmem = pl.BlockSpec(memory_space=pltpu.VMEM)
    smem = pl.BlockSpec(memory_space=pltpu.SMEM)
    out = jax.ShapeDtypeStruct((2, nj, 128, 128), BF16)
    count = UPPER[-1][1] - UPPER[-1][0]
    late = [
        jax.ShapeDtypeStruct((count // 2, 128, 128), BF16),
        jax.ShapeDtypeStruct((16, 128), BF16),
        jax.ShapeDtypeStruct((count, 128, 128), F32),
    ]
    faces = pl.pallas_call(
        mega,
        in_specs=[hbm] * 4 + [vmem] * 5 + [smem] * 3,
        out_specs=[hbm] * 5,
        out_shape=[out] * 2 + late,
        scratch_shapes=[
            pltpu.VMEM((2, nj, 256, 256), BF16),
            pltpu.VMEM((2, nj, 256, 128), BF16),
            pltpu.VMEM((2, nj, 256, 128), BF16),
            pltpu.VMEM((2, nj, 256, 128), BF16),
            pltpu.VMEM((3, nj + 1, 128, 128), BF16),
            pltpu.VMEM((2, nj, 128, 128), BF16),
            pltpu.VMEM((3, nj + 1, 128, 128), BF16),
            pltpu.VMEM((nj, 128, 256), BF16),
            pltpu.VMEM((N, 128, 256), BF16),
            pltpu.VMEM((most, 128, 256), BF16),
            pltpu.VMEM((most, 256, 256), BF16),
            pltpu.VMEM((2, nj, 128, 128), BF16),
            pltpu.VMEM((2, nj, 128, 128), BF16),
            pltpu.VMEM((nj // 2, 128, 128), BF16),
            pltpu.VMEM((nj // 2, 128, 128), BF16),
            pltpu.VMEM((len(LOWER + UPPER), 16, 128), BF16),
            pltpu.VMEM((len(LOWER + UPPER), 16, 128), BF16),
            pltpu.VMEM((high, 128, 256), BF16),
            pltpu.VMEM((high, 128, 256), BF16),
            pltpu.VMEM((high, 128, 128), F32),
            pltpu.SemaphoreType.DMA((3,)),
            pltpu.SemaphoreType.DMA((21,)),
            pltpu.SemaphoreType.DMA((10,)),
            pltpu.SemaphoreType.DMA((17,)),
            pltpu.SemaphoreType.DMA((17,)),
        ],
        compiler_params=pltpu.CompilerParams(
            collective_id=0, has_side_effects=True, vmem_limit_bytes=60 << 20
        ),
        name="mega",
    )(
        cell_matrix, cell_interp, x_face_interp, y_face_interp,
        x_coupling, y_coupling, cell_skel, x_face_skel, y_face_skel,
        cell_rank, x_face_rank, y_face_rank,
    )
    return pl.pallas_call(
        finish,
        in_specs=[hbm] * 5,
        out_specs=[hbm] * 2,
        out_shape=[out] * 2,
        scratch_shapes=[
            pltpu.VMEM((2, 2, nj, 128, 128), BF16),
            pltpu.VMEM(late[0].shape, BF16),
            pltpu.VMEM(late[1].shape, BF16),
            pltpu.VMEM(late[2].shape, F32),
            pltpu.SemaphoreType.DMA((7,)),
            pltpu.SemaphoreType.DMA((5,)),
        ],
        compiler_params=pltpu.CompilerParams(vmem_limit_bytes=60 << 20),
        name="finish",
    )(*faces)


def solution(mesh):
    cells, face, one = P("gx", "yz", None, None), P("gx", "yz", None), P("gx", "yz")
    return jax.shard_map(
        body,
        mesh=mesh,
        in_specs=(cells, face, face, cells, face, one, cells, face, one, cells, face, one),
        out_specs=(cells, cells),
        check_vma=False,
    )
```

```python
import jax
import jax.numpy as jnp
from jax import lax
from jax.experimental import pallas as pl
from jax.experimental.pallas import tpu as pltpu
from jax.sharding import PartitionSpec as P

F32, BF16 = jnp.float32, jnp.bfloat16
ROWS = (((1,), (1,)), ((), ()))
N = 16
LOWER = ((0, 4), (4, 18))
UPPER = ((18, 22), (22, 28), (28, 32))


def dot(a, b):
    return jnp.dot(a, b, preferred_element_type=F32)


def dot_t(a, b):
    return lax.dot_general(a, b, ROWS, preferred_element_type=F32)


def basis_of(skel, rank, interp, rows):
    one, zero = jnp.ones((), BF16), jnp.zeros((), BF16)
    slots = lax.broadcasted_iota(jnp.int32, (1, 128), 1)
    live = slots < rank
    marked = jnp.where(live, skel, -1).astype(F32).astype(BF16)
    picked = rows == jnp.broadcast_to(marked, (256, 128))
    kept = jnp.where(jnp.broadcast_to(live, (256, 128)), interp, zero)
    turned = jnp.where(picked, one, kept).T
    most = turned[:16]
    for k in range(1, 8):
        most = jnp.maximum(most, turned[16 * k : 16 * k + 16])
    most = jnp.max(most.astype(F32), axis=0, keepdims=True)
    least = jnp.where(most > 0.5, 0.5, -1.0).astype(BF16)
    return jnp.where(turned > jnp.broadcast_to(least, (128, 256)), turned, zero)


def mega(
    matrix_hbm, cell_hbm, x_hbm, y_hbm,
    x_conduct_hbm, y_conduct_hbm, cell_skel_hbm, x_skel_hbm, y_skel_hbm, cell_rank_hbm, x_rank_hbm, y_rank_hbm,
    x_out, y_out, late_packed, late_lines, late_part,
    x_conduct, y_conduct, cell_skel, x_skel, y_skel, cell_rank, x_rank, y_rank,
    matrix, interp, x_interp, y_interp, tops, bottoms, schurs, x_basis, basis, inner, face,
    x_face, y_face, packed, packed_in, diagonals, diagonals_in, lifted, lifted_in, partial,
    small_sem, late_sem, in_sem, out_sem, send_sem, recv_sem,
):
    gx, yz = lax.axis_index("gx"), lax.axis_index("yz")
    gxs, yzs = lax.axis_size("gx"), lax.axis_size("yz")
    nj = cell_skel_hbm.shape[1]
    has_down, has_up = gx > 0, gx < gxs - 1
    has_left, has_right = yz > 0, yz < yzs - 1

    lower, upper = [range(*ends) for ends in LOWER], [range(*ends) for ends in UPPER]
    ranges = lower + upper
    low = range(lower[0].start, lower[-1].stop)
    high = range(upper[0].start, upper[-1].stop)
    halves = [range(k, k + N) for k in range(0, nj, N)]

    def cut(cols):
        return pl.ds(cols.start, len(cols))

    barrier = pltpu.get_barrier_semaphore()
    for there, device in (
        (has_down, {"gx": gx - 1}),
        (has_up, {"gx": gx + 1}),
        (has_left, {"yz": yz - 1}),
        (has_right, {"yz": yz + 1}),
    ):

        @pl.when(there)
        def _(device=device):
            pl.semaphore_signal(barrier, inc=1, device_id=device, device_id_type=pl.DeviceIdType.MESH)

    copies = {}

    def load(kind, row, cols):
        src, dst = {
            "m": (matrix_hbm, matrix), "c": (cell_hbm, interp), "x": (x_hbm, x_interp), "y": (y_hbm, y_interp)
        }[kind]
        copy = pltpu.make_async_copy(src.at[row, cut(cols)], dst.at[row, cut(cols)], in_sem.at[len(copies)])
        copy.start()
        copies[kind, row, cols] = copy

    def loaded(kind, row, cols):
        copies[kind, row, cols].wait()

    small = []

    def load_small(*pairs):
        for src, dst in pairs:
            small.append(pltpu.make_async_copy(src, dst, small_sem.at[len(small)]))
            small[-1].start()

    load_small(
        (cell_skel_hbm, cell_skel), (cell_rank_hbm, cell_rank), (x_skel_hbm, x_skel), (x_rank_hbm, x_rank),
        (x_conduct_hbm, x_conduct),
    )
    for k, cols in enumerate(upper):
        if k < len(lower):
            load("c", 0, lower[k])
        load("c", 1, cols)
        load("x", 1, cols)
    load("m", 0, low)
    load("c", 0, high)
    load("m", 0, high)
    unknowns = lax.broadcasted_iota(jnp.int32, (256, 128), 0).astype(F32).astype(BF16)
    down = lax.broadcasted_iota(jnp.int32, (128, 128), 0)
    across = lax.broadcasted_iota(jnp.int32, (128, 128), 1)

    made = []

    def remote(src, dst, device):
        at = len(made)
        made.append(at)
        return pltpu.make_async_remote_copy(
            src_ref=src, dst_ref=dst, send_sem=send_sem.at[at], recv_sem=recv_sem.at[at],
            device_id=device, device_id_type=pl.DeviceIdType.MESH,
        )

    lift = [
        remote(lifted.at[part], lifted_in.at[part], {"gx": gx + 1})
        for part in (pl.ds(cols.start - high.start, len(cols)) for cols in upper)
    ]
    top_copy = [remote(tops.at[0, cut(cols)], tops.at[2, cut(cols)], {"gx": gx - 1}) for cols in lower]
    pack_copy = []
    for k, cols in enumerate(ranges):
        pairs = pl.ds(cols.start // 2, len(cols) // 2)
        late = cols is upper[-1]
        pack_copy.append(
            (
                remote(packed.at[pairs], late_packed if late else packed_in.at[pairs], {"gx": gx - 1}),
                remote(diagonals.at[k], late_lines if late else diagonals_in.at[k], {"gx": gx - 1}),
            )
        )
    side_copy = [
        remote(ref.at[pl.ds(0, 2), 0], ref.at[pl.ds(0, 2), nj], {"yz": yz - 1}) for ref in (tops, schurs)
    ]

    outs = []

    def store(kind, row, cols):
        src, dst = {"x": (x_face, x_out), "y": (y_face, y_out)}[kind]
        copy = pltpu.make_async_copy(src.at[row, cut(cols)], dst.at[row, cut(cols)], out_sem.at[len(outs)])
        copy.start()
        outs.append(copy)

    def cell(row, j):
        return jnp.concatenate([tops[row, j], bottoms[row, j]], axis=1)

    def cell_bases(row, cols):
        for j in cols:
            value = basis_of(cell_skel[row, j : j + 1], cell_rank[row, j], interp[row, j], unknowns)
            tops[row, j] = value[:, :128]
            bottoms[row, j] = value[:, 128:]

    def cell_schurs(row, cols):
        for c, j in enumerate(cols):
            inner[c] = dot(cell(row, j), matrix[row, j]).astype(BF16)
        for c, j in enumerate(cols):
            schurs[row, j] = dot_t(inner[c], cell(row, j)).astype(BF16)

    def pack(k, blocks):
        lines = []
        for c, j in enumerate(range(ranges[k].start, ranges[k].stop, 2)):
            packed[j // 2] = jnp.where(down <= across, blocks(j), blocks(j + 1))
            lines.append(jnp.sum(jnp.where(down == across, blocks(j + 1).astype(F32), 0.0), axis=0, keepdims=True))
        lines.append(jnp.zeros((16 - len(lines), 128), F32))
        diagonals[k] = jnp.concatenate(lines, axis=0).astype(BF16)

    def unpack(k):
        for c, j in enumerate(range(ranges[k].start, ranges[k].stop, 2)):
            value = packed_in[j // 2]
            turned = value.T
            line = jnp.broadcast_to(diagonals_in[k, c : c + 1], (128, 128))
            schurs[2, j] = jnp.where(down <= across, value, turned)
            schurs[2, j + 1] = jnp.where(down == across, line, jnp.where(down > across, value, turned))

    def face_bases(row, cols, skel, rank, values, into):
        for c, j in enumerate(cols):
            into[c] = basis_of(skel[row, j : j + 1], rank[row, j], values[row, j], unknowns)

    def negative(conduct, row, j):
        return -conduct[row, j : j + 1].astype(F32)

    def face_links(row, cols, conduct, right):
        for c, j in enumerate(cols):
            scaled = (tops[right(j)].astype(F32) * negative(conduct, row, j)).astype(BF16)
            link = dot_t(bottoms[row, j], scaled).astype(BF16)
            face[c, :128, :128] = schurs[row, j]
            face[c, :128, 128:] = link
            face[c, 128:, :128] = link.T

    def face_ends(row, cols, right, bases, out, base=0):
        for c, j in enumerate(cols):
            face[base + c, 128:, 128:] = schurs[right(j)]
        for c, j in enumerate(cols):
            inner[c] = dot(bases[base + c], face[base + c]).astype(BF16)
        for c, j in enumerate(cols):
            out[row, j] = dot_t(bases[base + c], inner[c]).astype(BF16)

    def lift_out(cols):
        for j in cols:
            value = basis_of(x_skel[1, j : j + 1], x_rank[1, j], x_interp[1, j], unknowns)
            x_basis[j] = value
            lifted[j - high.start, :, :128] = value[:, 128:]
        for j in cols:
            carried = dot(x_basis[j, :, :128], bottoms[1, j]) * negative(x_conduct, 1, j)
            lifted[j - high.start, :, 128:] = carried.astype(BF16)

    def lift_back(cols):
        for c, j in enumerate(cols):
            both = jnp.concatenate([schurs[0, j], tops[0, j]], axis=1)
            inner[c] = dot(lifted_in[j - high.start, :, :128], both).astype(BF16)
        for c, j in enumerate(cols):
            here = lifted_in[j - high.start]
            value = dot_t(here, inner[c]) + dot_t(inner[c, :, 128:], here[:, 128:])
            face[c, :128, :128] = value.astype(BF16)

    def own_part(cols):
        for c, j in enumerate(cols):
            inner[c, :, :128] = dot(x_basis[j, :, :128], schurs[1, j]).astype(BF16)
        for c, j in enumerate(cols):
            partial[j - high.start] = dot_t(x_basis[j, :, :128], inner[c, :, :128])

    def send(k):
        for copy in pack_copy[k]:
            pl.when(has_down)(copy.start)

    def received(k):
        for copy in pack_copy[k]:
            pl.when(has_up)(copy.wait_recv)

    count = sum(x.astype(jnp.int32) for x in (has_down, has_up, has_left, has_right))
    for copy in small:
        copy.wait()
    for k, cols in enumerate(upper):
        if k < len(lower):
            loaded("c", 0, lower[k])
            cell_bases(0, lower[k])
            if k == 0:
                pl.semaphore_wait(barrier, count)
            pl.when(has_down)(top_copy[k].start)
        loaded("c", 1, cols)
        loaded("x", 1, cols)
        cell_bases(1, cols)
        lift_out(cols)
        pl.when(has_up)(lift[k].start)
    load("c", 1, low)
    load("m", 1, low)
    load("m", 1, high)
    for cols in halves:
        load("x", 0, cols)
    for cols in halves:
        load("y", 0, cols)
        load("y", 1, cols)
    load("x", 1, low)
    early = len(small)
    load_small((y_skel_hbm, y_skel), (y_rank_hbm, y_rank), (y_conduct_hbm, y_conduct))
    loaded("m", 0, low)
    cell_schurs(0, low)
    for k in range(len(lower)):
        pack(k, lambda j: schurs[0, j])
        send(k)
    loaded("c", 0, high)
    cell_bases(0, high)
    loaded("m", 0, high)
    cell_schurs(0, high)
    loaded("c", 1, low)
    cell_bases(1, low)
    loaded("m", 1, low)
    cell_schurs(1, low)
    for copy in side_copy:
        pl.when(has_left)(copy.start)
    loaded("m", 1, high)
    cell_schurs(1, high)

    @pl.when(jnp.logical_not(has_right))
    def _():
        for row in range(2):
            tops[row, nj] = jnp.zeros((128, 128), BF16)
            schurs[row, nj] = jnp.zeros((128, 128), BF16)

    @pl.when(jnp.logical_not(has_up))
    def _():
        tops[2] = jnp.zeros(tops.shape[1:], BF16)
        packed_in[...] = jnp.zeros_like(packed_in)
        diagonals_in[...] = jnp.zeros_like(diagonals_in)

    def own_faces(row, cols, kind):
        loaded(kind, row, cols)
        if kind == "x":
            right = lambda j: (1, j)
            face_links(row, cols, x_conduct, right)
            face_bases(row, cols, x_skel, x_rank, x_interp, basis)
            face_ends(row, cols, right, basis, x_face)
        else:
            right = lambda j: (row, j + 1)
            face_links(row, cols, y_conduct, right)
            face_bases(row, cols, y_skel, y_rank, y_interp, basis)
            face_ends(row, cols, right, basis, y_face)
        store(kind, row, cols)

    def answer(k):
        @pl.when(has_down)
        def _():
            lift[k].wait_recv()
            cols = upper[k]
            lift_back(cols)
            pack(len(lower) + k, lambda j: face[j - cols.start, :128, :128])
            for copy in pack_copy[len(lower) + k]:
                copy.start()

    for cols in halves:
        own_faces(0, cols, "x")
    for copy in small[early:]:
        copy.wait()
    own_faces(0, halves[0], "y")
    own_faces(1, halves[0], "y")
    answer(0)
    for copy in side_copy:
        pl.when(has_right)(copy.wait_recv)
    own_faces(0, halves[1], "y")
    own_faces(1, halves[1], "y")
    answer(1)
    own_part(high)
    loaded("x", 1, low)
    face_bases(1, low, x_skel, x_rank, x_interp, x_basis)
    for copy in top_copy:
        pl.when(has_up)(copy.wait_recv)
    face_links(1, low, x_conduct, lambda j: (2, j))
    last = pl.ds(upper[-1].start - high.start, len(upper[-1]))
    part_copy = pltpu.make_async_copy(partial.at[last], late_part, late_sem.at[0])
    part_copy.start()
    fill = [
        pltpu.make_async_copy(packed_in.at[pl.ds(0, len(upper[-1]) // 2)], late_packed, late_sem.at[1]),
        pltpu.make_async_copy(diagonals_in.at[0], late_lines, late_sem.at[2]),
    ]

    @pl.when(jnp.logical_not(has_up))
    def _():
        for copy in fill:
            copy.start()
        for copy in fill:
            copy.wait()

    for k, cols in enumerate(lower):
        if k == len(lower) - 1:
            answer(len(upper) - 1)
        received(k)
        unpack(k)
        face_ends(1, cols, lambda j: (2, j), x_basis, x_face, cols.start)
        store("x", 1, cols)
    for k, cols in enumerate(upper[:-1], len(lower)):
        received(k)
        unpack(k)
        for j in cols:
            x_face[1, j] = (partial[j - high.start] + schurs[2, j].astype(F32)).astype(BF16)
        store("x", 1, cols)
    part_copy.wait()
    received(len(ranges) - 1)
    for copy in outs:
        copy.wait()
    for copy in top_copy + [copy for pair in pack_copy for copy in pair]:
        pl.when(has_down)(copy.wait_send)
    for copy in lift:
        pl.when(has_up)(copy.wait_send)
    for copy in side_copy:
        pl.when(has_left)(copy.wait_send)


def finish(x_in, y_in, packed_in, lines_in, part_in, x_out, y_out, held, packed, lines, part, in_sem, out_sem):
    first, stop = UPPER[-1]
    early, late = pl.ds(0, first), pl.ds(first, stop - first)
    pieces = [
        (y_in.at[0], held.at[1, 0], y_out.at[0]),
        (y_in.at[1], held.at[1, 1], y_out.at[1]),
        (x_in.at[0], held.at[0, 0], x_out.at[0]),
        (x_in.at[1, early], held.at[0, 1, early], x_out.at[1, early]),
    ]
    arrive = [pltpu.make_async_copy(src, here, in_sem.at[k]) for k, (src, here, _) in enumerate(pieces)]
    leave = [pltpu.make_async_copy(here, dst, out_sem.at[k]) for k, (_, here, dst) in enumerate(pieces)]
    for src, here in ((packed_in, packed), (lines_in, lines), (part_in, part)):
        arrive.append(pltpu.make_async_copy(src, here, in_sem.at[len(arrive)]))
    for copy in arrive:
        copy.start()
    for before, after in zip(arrive, leave):
        before.wait()
        after.start()
    for copy in arrive[len(leave) :]:
        copy.wait()
    down = lax.broadcasted_iota(jnp.int32, (128, 128), 0)
    across = lax.broadcasted_iota(jnp.int32, (128, 128), 1)
    for c in range((stop - first) // 2):
        value = packed[c]
        turned = value.T
        line = jnp.broadcast_to(lines[c : c + 1], (128, 128))
        one = jnp.where(down <= across, value, turned)
        two = jnp.where(down == across, line, jnp.where(down > across, value, turned))
        for k, answer in ((2 * c, one), (2 * c + 1, two)):
            held[0, 1, first + k] = (part[k] + answer.astype(F32)).astype(BF16)
    leave.append(pltpu.make_async_copy(held.at[0, 1, late], x_out.at[1, late], out_sem.at[len(leave)]))
    leave[-1].start()
    for copy in leave:
        copy.wait()


def body(*args):
    (
        cell_matrix, x_coupling, y_coupling, cell_interp, cell_skel, cell_rank,
        x_face_interp, x_face_skel, x_face_rank, y_face_interp, y_face_skel, y_face_rank,
    ) = args
    nj = cell_skel.shape[1]
    low, high = LOWER[-1][1] - LOWER[0][0], UPPER[-1][1] - UPPER[0][0]
    most = max(N, low, high)
    hbm = pl.BlockSpec(memory_space=pl.ANY)
    out = jax.ShapeDtypeStruct((2, nj, 128, 128), BF16)
    count = UPPER[-1][1] - UPPER[-1][0]
    late = [
        jax.ShapeDtypeStruct((count // 2, 128, 128), BF16),
        jax.ShapeDtypeStruct((16, 128), BF16),
        jax.ShapeDtypeStruct((count, 128, 128), F32),
    ]
    faces = pl.pallas_call(
        mega,
        in_specs=[hbm] * 12,
        out_specs=[hbm] * 5,
        out_shape=[out] * 2 + late,
        scratch_shapes=[
            pltpu.VMEM((2, nj, 128), BF16),
            pltpu.VMEM((2, nj, 128), BF16),
            pltpu.VMEM((2, nj, 128), jnp.int32),
            pltpu.VMEM((2, nj, 128), jnp.int32),
            pltpu.VMEM((2, nj, 128), jnp.int32),
            pltpu.SMEM((2, nj), jnp.int32),
            pltpu.SMEM((2, nj), jnp.int32),
            pltpu.SMEM((2, nj), jnp.int32),
            pltpu.VMEM((2, nj, 256, 256), BF16),
            pltpu.VMEM((2, nj, 256, 128), BF16),
            pltpu.VMEM((2, nj, 256, 128), BF16),
            pltpu.VMEM((2, nj, 256, 128), BF16),
            pltpu.VMEM((3, nj + 1, 128, 128), BF16),
            pltpu.VMEM((2, nj, 128, 128), BF16),
            pltpu.VMEM((3, nj + 1, 128, 128), BF16),
            pltpu.VMEM((nj, 128, 256), BF16),
            pltpu.VMEM((N, 128, 256), BF16),
            pltpu.VMEM((most, 128, 256), BF16),
            pltpu.VMEM((most, 256, 256), BF16),
            pltpu.VMEM((2, nj, 128, 128), BF16),
            pltpu.VMEM((2, nj, 128, 128), BF16),
            pltpu.VMEM((nj // 2, 128, 128), BF16),
            pltpu.VMEM((nj // 2, 128, 128), BF16),
            pltpu.VMEM((len(LOWER + UPPER), 16, 128), BF16),
            pltpu.VMEM((len(LOWER + UPPER), 16, 128), BF16),
            pltpu.VMEM((high, 128, 256), BF16),
            pltpu.VMEM((high, 128, 256), BF16),
            pltpu.VMEM((high, 128, 128), F32),
            pltpu.SemaphoreType.DMA((8,)),
            pltpu.SemaphoreType.DMA((3,)),
            pltpu.SemaphoreType.DMA((21,)),
            pltpu.SemaphoreType.DMA((10,)),
            pltpu.SemaphoreType.DMA((17,)),
            pltpu.SemaphoreType.DMA((17,)),
        ],
        compiler_params=pltpu.CompilerParams(
            collective_id=0, has_side_effects=True, vmem_limit_bytes=60 << 20
        ),
        name="mega",
    )(
        cell_matrix, cell_interp, x_face_interp, y_face_interp,
        x_coupling, y_coupling, cell_skel, x_face_skel, y_face_skel,
        cell_rank, x_face_rank, y_face_rank,
    )
    return pl.pallas_call(
        finish,
        in_specs=[hbm] * 5,
        out_specs=[hbm] * 2,
        out_shape=[out] * 2,
        scratch_shapes=[
            pltpu.VMEM((2, 2, nj, 128, 128), BF16),
            pltpu.VMEM(late[0].shape, BF16),
            pltpu.VMEM(late[1].shape, BF16),
            pltpu.VMEM(late[2].shape, F32),
            pltpu.SemaphoreType.DMA((7,)),
            pltpu.SemaphoreType.DMA((5,)),
        ],
        compiler_params=pltpu.CompilerParams(vmem_limit_bytes=60 << 20),
        name="finish",
    )(*faces)


def solution(mesh):
    cells, face, one = P("gx", "yz", None, None), P("gx", "yz", None), P("gx", "yz")
    return jax.shard_map(
        body,
        mesh=mesh,
        in_specs=(cells, face, face, cells, face, one, cells, face, one, cells, face, one),
        out_specs=(cells, cells),
        check_vma=False,
    )
```

```python
import jax
import jax.numpy as jnp
from jax import lax
from jax.experimental import pallas as pl
from jax.experimental.pallas import tpu as pltpu
from jax.sharding import PartitionSpec as P

F32, BF16 = jnp.float32, jnp.bfloat16
ROWS = (((1,), (1,)), ((), ()))
N = 16
LOWER = ((0, 4), (4, 18))
UPPER = ((18, 22), (22, 28), (28, 32))


def dot(a, b):
    return jnp.dot(a, b, preferred_element_type=F32)


def dot_t(a, b):
    return lax.dot_general(a, b, ROWS, preferred_element_type=F32)


def basis_of(skel, rank, interp, rows):
    one, zero = jnp.ones((), BF16), jnp.zeros((), BF16)
    slots = lax.broadcasted_iota(jnp.int32, (1, 128), 1)
    live = slots < rank
    marked = jnp.where(live, skel, -1).astype(F32).astype(BF16)
    picked = rows == jnp.broadcast_to(marked, (256, 128))
    kept = jnp.where(jnp.broadcast_to(live, (256, 128)), interp, zero)
    turned = jnp.where(picked, one, kept).T
    most = turned[:16]
    for k in range(1, 8):
        most = jnp.maximum(most, turned[16 * k : 16 * k + 16])
    most = jnp.max(most.astype(F32), axis=0, keepdims=True)
    least = jnp.where(most > 0.5, 0.5, -1.0).astype(BF16)
    return jnp.where(turned > jnp.broadcast_to(least, (128, 256)), turned, zero)


def mega(
    matrix_hbm, cell_hbm, x_hbm, y_hbm,
    x_conduct_hbm, y_conduct_hbm, cell_skel_hbm, x_skel_hbm, y_skel_hbm, cell_rank_hbm, x_rank_hbm, y_rank_hbm,
    x_out, y_out, late_packed, late_lines, late_part,
    x_conduct, y_conduct, cell_skel, x_skel, y_skel, cell_rank, x_rank, y_rank,
    matrix, interp, x_interp, y_interp, tops, bottoms, schurs, x_basis, basis, inner, face,
    x_face, y_face, packed, packed_in, diagonals, diagonals_in, lifted, lifted_in, partial,
    small_sem, late_sem, in_sem, out_sem, send_sem, recv_sem,
):
    gx, yz = lax.axis_index("gx"), lax.axis_index("yz")
    gxs, yzs = lax.axis_size("gx"), lax.axis_size("yz")
    nj = cell_skel_hbm.shape[1]
    has_down, has_up = gx > 0, gx < gxs - 1
    has_left, has_right = yz > 0, yz < yzs - 1

    lower, upper = [range(*ends) for ends in LOWER], [range(*ends) for ends in UPPER]
    ranges = lower + upper
    low = range(lower[0].start, lower[-1].stop)
    high = range(upper[0].start, upper[-1].stop)
    halves = [range(k, k + N) for k in range(0, nj, N)]

    def cut(cols):
        return pl.ds(cols.start, len(cols))

    barrier = pltpu.get_barrier_semaphore()
    for there, device in (
        (has_down, {"gx": gx - 1}),
        (has_up, {"gx": gx + 1}),
        (has_left, {"yz": yz - 1}),
        (has_right, {"yz": yz + 1}),
    ):

        @pl.when(there)
        def _(device=device):
            pl.semaphore_signal(barrier, inc=1, device_id=device, device_id_type=pl.DeviceIdType.MESH)

    copies = {}

    def load(kind, row, cols):
        src, dst = {
            "m": (matrix_hbm, matrix), "c": (cell_hbm, interp), "x": (x_hbm, x_interp), "y": (y_hbm, y_interp)
        }[kind]
        copy = pltpu.make_async_copy(src.at[row, cut(cols)], dst.at[row, cut(cols)], in_sem.at[len(copies)])
        copy.start()
        copies[kind, row, cols] = copy

    def loaded(kind, row, cols):
        copies[kind, row, cols].wait()

    small = []

    def load_small(*pairs):
        for src, dst in pairs:
            small.append(pltpu.make_async_copy(src, dst, small_sem.at[len(small)]))
            small[-1].start()

    load_small((cell_skel_hbm, cell_skel), (cell_rank_hbm, cell_rank))
    first = len(small)
    for k, cols in enumerate(upper):
        if k < len(lower):
            load("c", 0, lower[k])
        if k == 0:
            load_small((x_skel_hbm, x_skel), (x_rank_hbm, x_rank), (x_conduct_hbm, x_conduct))
        load("c", 1, cols)
        load("x", 1, cols)
    load("m", 0, low)
    load("c", 0, high)
    load("m", 0, high)
    unknowns = lax.broadcasted_iota(jnp.int32, (256, 128), 0).astype(F32).astype(BF16)
    down = lax.broadcasted_iota(jnp.int32, (128, 128), 0)
    across = lax.broadcasted_iota(jnp.int32, (128, 128), 1)

    made = []

    def remote(src, dst, device):
        at = len(made)
        made.append(at)
        return pltpu.make_async_remote_copy(
            src_ref=src, dst_ref=dst, send_sem=send_sem.at[at], recv_sem=recv_sem.at[at],
            device_id=device, device_id_type=pl.DeviceIdType.MESH,
        )

    lift = [
        remote(lifted.at[part], lifted_in.at[part], {"gx": gx + 1})
        for part in (pl.ds(cols.start - high.start, len(cols)) for cols in upper)
    ]
    top_copy = [remote(tops.at[0, cut(cols)], tops.at[2, cut(cols)], {"gx": gx - 1}) for cols in lower]
    pack_copy = []
    for k, cols in enumerate(ranges):
        pairs = pl.ds(cols.start // 2, len(cols) // 2)
        late = cols is upper[-1]
        pack_copy.append(
            (
                remote(packed.at[pairs], late_packed if late else packed_in.at[pairs], {"gx": gx - 1}),
                remote(diagonals.at[k], late_lines if late else diagonals_in.at[k], {"gx": gx - 1}),
            )
        )
    side_copy = [
        remote(ref.at[pl.ds(0, 2), 0], ref.at[pl.ds(0, 2), nj], {"yz": yz - 1}) for ref in (tops, schurs)
    ]

    outs = []

    def store(kind, row, cols):
        src, dst = {"x": (x_face, x_out), "y": (y_face, y_out)}[kind]
        copy = pltpu.make_async_copy(src.at[row, cut(cols)], dst.at[row, cut(cols)], out_sem.at[len(outs)])
        copy.start()
        outs.append(copy)

    def cell(row, j):
        return jnp.concatenate([tops[row, j], bottoms[row, j]], axis=1)

    def cell_bases(row, cols):
        for j in cols:
            value = basis_of(cell_skel[row, j : j + 1], cell_rank[row, j], interp[row, j], unknowns)
            tops[row, j] = value[:, :128]
            bottoms[row, j] = value[:, 128:]

    def cell_schurs(row, cols):
        for c, j in enumerate(cols):
            inner[c] = dot(cell(row, j), matrix[row, j]).astype(BF16)
        for c, j in enumerate(cols):
            schurs[row, j] = dot_t(inner[c], cell(row, j)).astype(BF16)

    def pack(k, blocks):
        lines = []
        for c, j in enumerate(range(ranges[k].start, ranges[k].stop, 2)):
            packed[j // 2] = jnp.where(down <= across, blocks(j), blocks(j + 1))
            lines.append(jnp.sum(jnp.where(down == across, blocks(j + 1).astype(F32), 0.0), axis=0, keepdims=True))
        lines.append(jnp.zeros((16 - len(lines), 128), F32))
        diagonals[k] = jnp.concatenate(lines, axis=0).astype(BF16)

    def unpack(k):
        for c, j in enumerate(range(ranges[k].start, ranges[k].stop, 2)):
            value = packed_in[j // 2]
            turned = value.T
            line = jnp.broadcast_to(diagonals_in[k, c : c + 1], (128, 128))
            schurs[2, j] = jnp.where(down <= across, value, turned)
            schurs[2, j + 1] = jnp.where(down == across, line, jnp.where(down > across, value, turned))

    def face_bases(row, cols, skel, rank, values, into):
        for c, j in enumerate(cols):
            into[c] = basis_of(skel[row, j : j + 1], rank[row, j], values[row, j], unknowns)

    def negative(conduct, row, j):
        return -conduct[row, j : j + 1].astype(F32)

    def face_links(row, cols, conduct, right):
        for c, j in enumerate(cols):
            scaled = (tops[right(j)].astype(F32) * negative(conduct, row, j)).astype(BF16)
            link = dot_t(bottoms[row, j], scaled).astype(BF16)
            face[c, :128, :128] = schurs[row, j]
            face[c, :128, 128:] = link
            face[c, 128:, :128] = link.T

    def face_ends(row, cols, right, bases, out, base=0):
        for c, j in enumerate(cols):
            face[base + c, 128:, 128:] = schurs[right(j)]
        for c, j in enumerate(cols):
            inner[c] = dot(bases[base + c], face[base + c]).astype(BF16)
        for c, j in enumerate(cols):
            out[row, j] = dot_t(bases[base + c], inner[c]).astype(BF16)

    def lift_out(cols):
        for j in cols:
            value = basis_of(x_skel[1, j : j + 1], x_rank[1, j], x_interp[1, j], unknowns)
            x_basis[j] = value
            lifted[j - high.start, :, :128] = value[:, 128:]
        for j in cols:
            carried = dot(x_basis[j, :, :128], bottoms[1, j]) * negative(x_conduct, 1, j)
            lifted[j - high.start, :, 128:] = carried.astype(BF16)

    def lift_back(cols):
        for c, j in enumerate(cols):
            both = jnp.concatenate([schurs[0, j], tops[0, j]], axis=1)
            inner[c] = dot(lifted_in[j - high.start, :, :128], both).astype(BF16)
        for c, j in enumerate(cols):
            here = lifted_in[j - high.start]
            value = dot_t(here, inner[c]) + dot_t(inner[c, :, 128:], here[:, 128:])
            face[c, :128, :128] = value.astype(BF16)

    def own_part(cols):
        for c, j in enumerate(cols):
            inner[c, :, :128] = dot(x_basis[j, :, :128], schurs[1, j]).astype(BF16)
        for c, j in enumerate(cols):
            partial[j - high.start] = dot_t(x_basis[j, :, :128], inner[c, :, :128])

    def send(k):
        for copy in pack_copy[k]:
            pl.when(has_down)(copy.start)

    def received(k):
        for copy in pack_copy[k]:
            pl.when(has_up)(copy.wait_recv)

    count = sum(x.astype(jnp.int32) for x in (has_down, has_up, has_left, has_right))
    for copy in small[:first]:
        copy.wait()
    middle = len(small)
    for k, cols in enumerate(upper):
        if k < len(lower):
            loaded("c", 0, lower[k])
            cell_bases(0, lower[k])
            if k == 0:
                pl.semaphore_wait(barrier, count)
            pl.when(has_down)(top_copy[k].start)
        if k == 0:
            for copy in small[first:middle]:
                copy.wait()
        loaded("c", 1, cols)
        loaded("x", 1, cols)
        cell_bases(1, cols)
        lift_out(cols)
        pl.when(has_up)(lift[k].start)
    load("c", 1, low)
    load("m", 1, low)
    load("m", 1, high)
    for cols in halves:
        load("x", 0, cols)
    for cols in halves:
        load("y", 0, cols)
        load("y", 1, cols)
    load("x", 1, low)
    early = len(small)
    load_small((y_skel_hbm, y_skel), (y_rank_hbm, y_rank), (y_conduct_hbm, y_conduct))
    loaded("m", 0, low)
    cell_schurs(0, low)
    for k in range(len(lower)):
        pack(k, lambda j: schurs[0, j])
        send(k)
    loaded("c", 0, high)
    cell_bases(0, high)
    loaded("m", 0, high)
    cell_schurs(0, high)
    loaded("c", 1, low)
    cell_bases(1, low)
    loaded("m", 1, low)
    cell_schurs(1, low)
    for copy in side_copy:
        pl.when(has_left)(copy.start)
    loaded("m", 1, high)
    cell_schurs(1, high)

    @pl.when(jnp.logical_not(has_right))
    def _():
        for row in range(2):
            tops[row, nj] = jnp.zeros((128, 128), BF16)
            schurs[row, nj] = jnp.zeros((128, 128), BF16)

    @pl.when(jnp.logical_not(has_up))
    def _():
        tops[2] = jnp.zeros(tops.shape[1:], BF16)
        packed_in[...] = jnp.zeros_like(packed_in)
        diagonals_in[...] = jnp.zeros_like(diagonals_in)

    def own_faces(row, cols, kind):
        loaded(kind, row, cols)
        if kind == "x":
            right = lambda j: (1, j)
            face_links(row, cols, x_conduct, right)
            face_bases(row, cols, x_skel, x_rank, x_interp, basis)
            face_ends(row, cols, right, basis, x_face)
        else:
            right = lambda j: (row, j + 1)
            face_links(row, cols, y_conduct, right)
            face_bases(row, cols, y_skel, y_rank, y_interp, basis)
            face_ends(row, cols, right, basis, y_face)
        store(kind, row, cols)

    def answer(k):
        @pl.when(has_down)
        def _():
            lift[k].wait_recv()
            cols = upper[k]
            lift_back(cols)
            pack(len(lower) + k, lambda j: face[j - cols.start, :128, :128])
            for copy in pack_copy[len(lower) + k]:
                copy.start()

    for cols in halves:
        own_faces(0, cols, "x")
    for copy in small[early:]:
        copy.wait()
    own_faces(0, halves[0], "y")
    own_faces(1, halves[0], "y")
    answer(0)
    for copy in side_copy:
        pl.when(has_right)(copy.wait_recv)
    own_faces(0, halves[1], "y")
    own_faces(1, halves[1], "y")
    answer(1)
    own_part(high)
    loaded("x", 1, low)
    face_bases(1, low, x_skel, x_rank, x_interp, x_basis)
    for copy in top_copy:
        pl.when(has_up)(copy.wait_recv)
    face_links(1, low, x_conduct, lambda j: (2, j))
    last = pl.ds(upper[-1].start - high.start, len(upper[-1]))
    part_copy = pltpu.make_async_copy(partial.at[last], late_part, late_sem.at[0])
    part_copy.start()
    fill = [
        pltpu.make_async_copy(packed_in.at[pl.ds(0, len(upper[-1]) // 2)], late_packed, late_sem.at[1]),
        pltpu.make_async_copy(diagonals_in.at[0], late_lines, late_sem.at[2]),
    ]

    @pl.when(jnp.logical_not(has_up))
    def _():
        for copy in fill:
            copy.start()
        for copy in fill:
            copy.wait()

    for k, cols in enumerate(lower):
        if k == len(lower) - 1:
            answer(len(upper) - 1)
        received(k)
        unpack(k)
        face_ends(1, cols, lambda j: (2, j), x_basis, x_face, cols.start)
        store("x", 1, cols)
    for k, cols in enumerate(upper[:-1], len(lower)):
        received(k)
        unpack(k)
        for j in cols:
            x_face[1, j] = (partial[j - high.start] + schurs[2, j].astype(F32)).astype(BF16)
        store("x", 1, cols)
    part_copy.wait()
    received(len(ranges) - 1)
    for copy in outs:
        copy.wait()
    for copy in top_copy + [copy for pair in pack_copy for copy in pair]:
        pl.when(has_down)(copy.wait_send)
    for copy in lift:
        pl.when(has_up)(copy.wait_send)
    for copy in side_copy:
        pl.when(has_left)(copy.wait_send)


def finish(x_in, y_in, packed_in, lines_in, part_in, x_out, y_out, held, packed, lines, part, in_sem, out_sem):
    first, stop = UPPER[-1]
    early, late = pl.ds(0, first), pl.ds(first, stop - first)
    pieces = [
        (y_in.at[0], held.at[1, 0], y_out.at[0]),
        (y_in.at[1], held.at[1, 1], y_out.at[1]),
        (x_in.at[0], held.at[0, 0], x_out.at[0]),
        (x_in.at[1, early], held.at[0, 1, early], x_out.at[1, early]),
    ]
    arrive = [pltpu.make_async_copy(src, here, in_sem.at[k]) for k, (src, here, _) in enumerate(pieces)]
    leave = [pltpu.make_async_copy(here, dst, out_sem.at[k]) for k, (_, here, dst) in enumerate(pieces)]
    for src, here in ((packed_in, packed), (lines_in, lines), (part_in, part)):
        arrive.append(pltpu.make_async_copy(src, here, in_sem.at[len(arrive)]))
    for copy in arrive:
        copy.start()
    for before, after in zip(arrive, leave):
        before.wait()
        after.start()
    for copy in arrive[len(leave) :]:
        copy.wait()
    down = lax.broadcasted_iota(jnp.int32, (128, 128), 0)
    across = lax.broadcasted_iota(jnp.int32, (128, 128), 1)
    for c in range((stop - first) // 2):
        value = packed[c]
        turned = value.T
        line = jnp.broadcast_to(lines[c : c + 1], (128, 128))
        one = jnp.where(down <= across, value, turned)
        two = jnp.where(down == across, line, jnp.where(down > across, value, turned))
        for k, answer in ((2 * c, one), (2 * c + 1, two)):
            held[0, 1, first + k] = (part[k] + answer.astype(F32)).astype(BF16)
    leave.append(pltpu.make_async_copy(held.at[0, 1, late], x_out.at[1, late], out_sem.at[len(leave)]))
    leave[-1].start()
    for copy in leave:
        copy.wait()


def body(*args):
    (
        cell_matrix, x_coupling, y_coupling, cell_interp, cell_skel, cell_rank,
        x_face_interp, x_face_skel, x_face_rank, y_face_interp, y_face_skel, y_face_rank,
    ) = args
    nj = cell_skel.shape[1]
    low, high = LOWER[-1][1] - LOWER[0][0], UPPER[-1][1] - UPPER[0][0]
    most = max(N, low, high)
    hbm = pl.BlockSpec(memory_space=pl.ANY)
    out = jax.ShapeDtypeStruct((2, nj, 128, 128), BF16)
    count = UPPER[-1][1] - UPPER[-1][0]
    late = [
        jax.ShapeDtypeStruct((count // 2, 128, 128), BF16),
        jax.ShapeDtypeStruct((16, 128), BF16),
        jax.ShapeDtypeStruct((count, 128, 128), F32),
    ]
    faces = pl.pallas_call(
        mega,
        in_specs=[hbm] * 12,
        out_specs=[hbm] * 5,
        out_shape=[out] * 2 + late,
        scratch_shapes=[
            pltpu.VMEM((2, nj, 128), BF16),
            pltpu.VMEM((2, nj, 128), BF16),
            pltpu.VMEM((2, nj, 128), jnp.int32),
            pltpu.VMEM((2, nj, 128), jnp.int32),
            pltpu.VMEM((2, nj, 128), jnp.int32),
            pltpu.SMEM((2, nj), jnp.int32),
            pltpu.SMEM((2, nj), jnp.int32),
            pltpu.SMEM((2, nj), jnp.int32),
            pltpu.VMEM((2, nj, 256, 256), BF16),
            pltpu.VMEM((2, nj, 256, 128), BF16),
            pltpu.VMEM((2, nj, 256, 128), BF16),
            pltpu.VMEM((2, nj, 256, 128), BF16),
            pltpu.VMEM((3, nj + 1, 128, 128), BF16),
            pltpu.VMEM((2, nj, 128, 128), BF16),
            pltpu.VMEM((3, nj + 1, 128, 128), BF16),
            pltpu.VMEM((nj, 128, 256), BF16),
            pltpu.VMEM((N, 128, 256), BF16),
            pltpu.VMEM((most, 128, 256), BF16),
            pltpu.VMEM((most, 256, 256), BF16),
            pltpu.VMEM((2, nj, 128, 128), BF16),
            pltpu.VMEM((2, nj, 128, 128), BF16),
            pltpu.VMEM((nj // 2, 128, 128), BF16),
            pltpu.VMEM((nj // 2, 128, 128), BF16),
            pltpu.VMEM((len(LOWER + UPPER), 16, 128), BF16),
            pltpu.VMEM((len(LOWER + UPPER), 16, 128), BF16),
            pltpu.VMEM((high, 128, 256), BF16),
            pltpu.VMEM((high, 128, 256), BF16),
            pltpu.VMEM((high, 128, 128), F32),
            pltpu.SemaphoreType.DMA((8,)),
            pltpu.SemaphoreType.DMA((3,)),
            pltpu.SemaphoreType.DMA((21,)),
            pltpu.SemaphoreType.DMA((10,)),
            pltpu.SemaphoreType.DMA((17,)),
            pltpu.SemaphoreType.DMA((17,)),
        ],
        compiler_params=pltpu.CompilerParams(
            collective_id=0, has_side_effects=True, vmem_limit_bytes=60 << 20
        ),
        name="mega",
    )(
        cell_matrix, cell_interp, x_face_interp, y_face_interp,
        x_coupling, y_coupling, cell_skel, x_face_skel, y_face_skel,
        cell_rank, x_face_rank, y_face_rank,
    )
    return pl.pallas_call(
        finish,
        in_specs=[hbm] * 5,
        out_specs=[hbm] * 2,
        out_shape=[out] * 2,
        scratch_shapes=[
            pltpu.VMEM((2, 2, nj, 128, 128), BF16),
            pltpu.VMEM(late[0].shape, BF16),
            pltpu.VMEM(late[1].shape, BF16),
            pltpu.VMEM(late[2].shape, F32),
            pltpu.SemaphoreType.DMA((7,)),
            pltpu.SemaphoreType.DMA((5,)),
        ],
        compiler_params=pltpu.CompilerParams(vmem_limit_bytes=60 << 20),
        name="finish",
    )(*faces)


def solution(mesh):
    cells, face, one = P("gx", "yz", None, None), P("gx", "yz", None), P("gx", "yz")
    return jax.shard_map(
        body,
        mesh=mesh,
        in_specs=(cells, face, face, cells, face, one, cells, face, one, cells, face, one),
        out_specs=(cells, cells),
        check_vma=False,
    )
```
